32 devices in a mesh: group: 2 (over y), chan: 4 (over z), stat: 2 (over x), pol: 2 (over core).
Axes of the slice: x: 2, y: 2, z: 4, core: 2. Of those that a mesh axis runs over, the one named last changes fastest.
Arguments:
- voltages: bfloat16 [4, 16, 2, 19, 2, 4096], P(('group', 'stat'), 'chan', 'pol'), parts along dimension 0, may hold values from -6 to 6
- filter_taps: float32 [12, 4096], replicated, may hold values from -1.5 to 1.5
- beam_table: float32 [2, 16], replicated, may hold values from -4 to 4
- beam_index: int32 [500, 32], replicated, may hold values from 0 to 15
- block_owner: int32 [32], replicated, may hold values from 0 to 31, each once
Outputs:
- visibilities: float32 [64, 2, 64, 64], P(('group', 'chan'), None, ('stat', 'pol')), parts along dimension 0
- beams: float32 [1000, 2, 2, 8, 4096], P(('group', 'stat'), 'pol', None, None, 'chan'), parts along dimension 0
The draws below stay inside these ranges and needn't reach their ends.
There are 2 independent parts, one for each index of `group`. The reference program is written for one: setup_inputs(seed, part) draws one part's arguments, and reference() takes and returns one part's arrays. A program takes and returns all parts, laid end to end along the dimension named above; an argument that names none is the same for every part. Nothing has to cross between parts.
Inputs may be any that keep to these rules, and one draw needn't show every extreme that they name: `block_owner`: each of the 32 channel groups appears at exactly one position.
All inputs are finite; a program needn't handle non-finite values.
Results may differ from the reference program's by a relative error of at most 0.0095.
Values may be sent and summed in bfloat16 or wider, within the bound.
No kernel may reach another device: no remote copies, remote signals or barrier semaphores. Data moves between devices by JAX's collectives and lax.ppermute only.
A program may use at most 64 MiB of HBM per device.

```python
import math
import jax
import jax.numpy as jnp
from jax import lax

NFFT = 4096
TAPS = 12
AVG = 128
TABLE = 16
BEAMS = 500
FR = 8
BLOCKS = 19
SEC = 16
SECTIONS = 2
STATIONS = 32
INPUTS = 64
NAVG = 32


def plant(drawn, stream_key, low, largest):
    place = [jax.random.randint(jax.random.fold_in(stream_key, axis), (), 0, length) for axis, length in enumerate(drawn.shape)]
    longest = drawn.shape.index(max(drawn.shape))
    next_to = place[:longest] + [(place[longest] + 1) % drawn.shape[longest]] + place[longest + 1:]
    return drawn.at[tuple(place)].set(low).at[tuple(next_to)].set(largest)


def shard_levels(stream_key, dims, cuts, smallest, largest):
    def one(dim, parts):
        heights = jax.random.uniform(jax.random.fold_in(jax.random.fold_in(stream_key, 6), dim), (parts,), jnp.float32, smallest / len(cuts), largest / len(cuts))
        return jnp.repeat(jnp.exp(heights), dims[dim] // parts).reshape((-1,) + (1,) * (len(dims) - dim - 1))

    gain = one(*cuts[0])
    for cut in cuts[1:]:
        gain = gain * one(*cut)
    return gain


def scatter_about(key, dims, spread, bound, shards=(), held_as=jnp.bfloat16):
    entries = spread * jax.random.normal(key, dims, jnp.float32)
    if shards:
        entries = entries * shard_levels(key, dims, shards, -0.22, 0.18)
    return jnp.clip(entries, -bound, bound).astype(held_as)


def setup_inputs(seed: int = 0, part: int = 0) -> dict:
    streams_of = jax.random.split(jax.random.key(seed), 6)
    part_keys = jax.random.split(jax.random.fold_in(streams_of[5], part), 6)
    voltages = scatter_about(part_keys[0], (SECTIONS, SEC, 2, BLOCKS, 2, NFFT), 1.0, 6.0, ((0, 2), (1, 4), (2, 2)))
    filter_taps = scatter_about(streams_of[1], (TAPS, NFFT), 0.3, 1.5, (), jnp.float32)
    beam_table = scatter_about(streams_of[2], (2, TABLE), 1.0, 4.0, (), jnp.float32)
    beam_index = plant(jax.random.randint(streams_of[3], (BEAMS, STATIONS), 0, TABLE), jax.random.fold_in(streams_of[3], 1), 0, TABLE - 1).astype(jnp.int32)
    block_owner = jax.random.permutation(streams_of[4], NAVG).astype(jnp.int32)
    return {"voltages": voltages, "filter_taps": filter_taps, "beam_table": beam_table, "beam_index": beam_index, "block_owner": block_owner}


def reference(voltages, filter_taps, beam_table, beam_index, block_owner):

    def channelise(section):
        samples = section.astype(jnp.float32)
        filtered = jnp.zeros((SEC, 2, FR, 2, NFFT), jnp.float32)
        for tap_index in range(TAPS):
            filtered = filtered + filter_taps[tap_index] * samples[:, :, tap_index:tap_index + FR]
        spectrum = jnp.fft.fft(filtered[:, :, :, 0] + 1j * filtered[:, :, :, 1], axis=-1, norm='ortho')
        stacked = jnp.stack([jnp.real(spectrum), jnp.imag(spectrum)], axis=2)
        return stacked.astype(jnp.bfloat16)
    spectra = lax.map(channelise, voltages)
    blocked = spectra.reshape(SECTIONS, SEC, 2, 2, FR, NAVG, AVG)
    ordered = jnp.take(blocked, block_owner, axis=5).reshape(SECTIONS, SEC, 2, 2, FR, NFFT)
    inputs = jnp.transpose(ordered, (0, 2, 1, 3, 4, 5)).reshape(INPUTS, 2, FR, NFFT // AVG, AVG)
    channel_groups = jnp.moveaxis(inputs, 3, 0)

    def average(channel_group):
        own_rows = channel_group.reshape(INPUTS, 2 * FR * AVG)
        rotated = jnp.concatenate([-channel_group[:, 1:2], channel_group[:, 0:1]], axis=1).reshape(INPUTS, 2 * FR * AVG)
        real_part = jnp.dot(own_rows, own_rows.T, preferred_element_type=jnp.float32)
        imag_part = jnp.dot(own_rows, rotated.T, preferred_element_type=jnp.float32)
        return jnp.stack([real_part, imag_part], axis=0) * (1.0 / (FR * AVG))
    visibilities = lax.map(average, channel_groups)
    weights = (beam_table[:, beam_index] * (1.0 / math.sqrt(STATIONS))).astype(jnp.bfloat16)
    stations = ordered.reshape(STATIONS, 2, 2, FR * NFFT)

    def form_beams(polarity):
        real_in = stations[:, polarity, 0]
        imag_in = stations[:, polarity, 1]
        real_out = jnp.dot(weights[0], real_in, preferred_element_type=jnp.float32) - jnp.dot(weights[1], imag_in, preferred_element_type=jnp.float32)
        imag_out = jnp.dot(weights[1], real_in, preferred_element_type=jnp.float32) + jnp.dot(weights[0], imag_in, preferred_element_type=jnp.float32)
        return jnp.stack([real_out, imag_out], axis=1)
    beams = jnp.stack([form_beams(0), form_beams(1)], axis=1).reshape(BEAMS, 2, 2, FR, NFFT)
    return (visibilities, beams)
```

```python
import functools, math
import jax, jax.numpy as jnp, numpy as np
from jax import lax
from jax.experimental import pallas as pl
from jax.experimental.pallas import tpu as pltpu
from jax.sharding import PartitionSpec as P

LANES = 128
HALF = 4

def dft_parts(rows, cols, length):
    phase = np.outer(np.arange(rows), np.arange(cols)) % length * (2.0 * np.pi / length)
    return np.cos(phase), np.sin(phase)


def channel_tables(nfft, frames, groups):
    depth = nfft // LANES
    per_group = LANES // depth
    cosine, sine = dft_parts(depth, depth, depth)
    pair = np.stack([np.stack([cosine, sine], -1), np.stack([-sine, cosine], -1)])
    first = np.einsum("akrc,fg->afkgrc", pair, np.eye(HALF))
    first = first.reshape(2 * HALF * depth, HALF * depth * 2)
    turn_cos, turn_sin = dft_parts(depth, LANES, nfft)
    cosine, sine = dft_parts(LANES, LANES, LANES)
    order = (np.arange(groups)[None, :] * per_group + np.arange(per_group)[:, None]).reshape(-1)
    cosine, sine = cosine[order] / math.sqrt(nfft), sine[order] / math.sqrt(nfft)
    second = np.concatenate([np.concatenate([cosine, sine], 1), np.concatenate([-sine, cosine], 1)], 0)
    spread = np.einsum("qr,fg,kl->qfkgrl", np.eye(per_group), np.eye(HALF), np.eye(depth))
    spread = spread.reshape(per_group * HALF * depth, HALF * per_group * depth)
    bf = lambda x: jnp.asarray(x, jnp.bfloat16)
    return bf(first), jnp.asarray(np.stack([turn_cos, turn_sin]), jnp.float32), bf(second), bf(spread)


def channel_kernel(owners, owner_ref, volt_ref, taps_ref, first_ref, turn_ref, second_ref, spread_ref, *rest):
    outs = rest[:owners]
    volts, tap_rows, first, turn, second, spread, filt, wide, pick, sems = rest[owners:]
    stations, blocks, rows, _ = volt_ref.shape
    taps = taps_ref.shape[0]
    frames = blocks - taps + 1
    halves = frames // HALF
    depth = rows // 2
    groups = owner_ref.shape[0]
    width = groups // owners
    quads = LANES // depth
    span = HALF * depth
    here = lax.axis_index("chan")
    copies = []
    for s in range(stations):
        copies.append(pltpu.make_async_copy(volt_ref.at[s], volts.at[s], sems.at[s]))
    consts = []
    for i, (src, dst) in enumerate([(first_ref, first), (turn_ref, turn), (second_ref, second), (spread_ref, spread)]):
        consts.append(pltpu.make_async_copy(src, dst, sems.at[stations + i]))
    for c in copies + consts:
        c.start()

    sub = lax.broadcasted_iota(jnp.int32, (8, LANES), 0)
    for t in range(taps):
        for m in range(rows // 8):
            parts = [jnp.broadcast_to(taps_ref[t : t + 1, pl.ds((4 * m + i) * LANES, LANES)], (8, LANES)) for i in range(4)]
            low = jnp.where(sub < 2, parts[0], parts[1])
            high = jnp.where(sub < 6, parts[2], parts[3])
            tap_rows[t, pl.ds(8 * m, 8), :] = jnp.where(sub < 4, low, high)

    sc = 2 * stations
    lane = lax.broadcasted_iota(jnp.int32, (sc, sc * groups), 1)
    base = lax.broadcasted_iota(jnp.int32, (sc, sc * groups), 0) * groups
    for k in range(owners):
        for j in range(width):
            g = owner_ref[(here ^ k) * width + j]
            p = (k * width + j) * sc
            pick[pl.ds(p, sc), :] = jnp.where(lane == base + g, 1.0, 0.0).astype(jnp.bfloat16)

    step = 16
    for s in range(stations):
        copies[s].wait()

        def fir(m, carry, s=s):
            at = pl.multiple_of(m * step, step)
            x = [volts[s, b, pl.ds(at, step), :].astype(jnp.float32) for b in range(blocks)]
            w = [tap_rows[t, pl.ds(at, step), :] for t in range(taps)]
            for f in range(frames):
                total = w[0] * x[f]
                for t in range(1, taps):
                    total = total + w[t] * x[f + t]
                row = pl.multiple_of((f % HALF) * rows + at, step)
                filt[s, pl.ds(row, step), pl.ds((f // HALF) * LANES, LANES)] = total.astype(jnp.bfloat16)
            return carry

        lax.fori_loop(0, rows // step, fir, 0)

    for c in consts:
        c.wait()
    f32 = jnp.float32
    cosine = jnp.concatenate([turn[0]] * HALF, 0)
    sine = jnp.concatenate([turn[1]] * HALF, 0)
    for s in range(stations):
        y = jnp.dot(first[...], filt[s], preferred_element_type=f32)
        re, im = y[:span], y[span:]
        turned = []
        for h in range(halves):
            a, b = re[:, h * LANES : (h + 1) * LANES], im[:, h * LANES : (h + 1) * LANES]
            turned.append(jnp.concatenate([a * cosine + b * sine, b * cosine - a * sine], 1))
        turned = jnp.concatenate(turned, 0).astype(jnp.bfloat16)
        z = lax.dot_general(second[...], turned, (((1,), (1,)), ((), ())), preferred_element_type=f32).astype(jnp.bfloat16)
        for c in range(2):
            for q in range(quads):
                for h in range(halves):
                    wide[h, pl.ds((s * 2 + c) * groups, groups), pl.ds(q * LANES, LANES)] = z[
                        c * quads * groups + q * groups : c * quads * groups + (q + 1) * groups, h * LANES : (h + 1) * LANES
                    ]
    for h in range(halves):
        y = jnp.dot(wide[h], spread[...], preferred_element_type=f32).astype(jnp.bfloat16)
        z = jnp.dot(pick[...], y, preferred_element_type=f32)
        for k in range(owners):
            for j in range(width):
                for f in range(HALF):
                    p = (k * width + j) * sc
                    outs[k][pl.ds((h * HALF + f) * sc, sc), pl.ds(j * LANES, LANES)] = z[
                        p : p + sc, f * LANES : (f + 1) * LANES
                    ].astype(jnp.bfloat16)


def channelise(voltages, filter_taps, block_owner, owners):
    _, stations, _, blocks, _, nfft = voltages.shape
    taps = filter_taps.shape[0]
    frames = blocks - taps + 1
    groups = block_owner.shape[0]
    depth = nfft // LANES
    volts = voltages.reshape(stations, blocks, 2, depth, LANES).transpose(0, 1, 3, 2, 4).reshape(stations, blocks, 2 * depth, LANES)
    first, turn, second, spread = channel_tables(nfft, frames, groups)
    sc = 2 * stations
    width = groups // owners
    anyspec = pl.BlockSpec(memory_space=pl.ANY)
    bf = jnp.bfloat16
    return pl.pallas_call(
        functools.partial(channel_kernel, owners),
        out_shape=[jax.ShapeDtypeStruct((frames * sc, width * LANES), bf)] * owners,
        in_specs=[pl.BlockSpec(memory_space=pltpu.SMEM), anyspec, pl.BlockSpec(memory_space=pltpu.VMEM)] + [anyspec] * 4,
        out_specs=[pl.BlockSpec(memory_space=pltpu.VMEM)] * owners,
        scratch_shapes=[
            pltpu.VMEM(volts.shape, bf),
            pltpu.VMEM((taps, 2 * depth, LANES), jnp.float32),
            pltpu.VMEM(first.shape, bf),
            pltpu.VMEM(turn.shape, jnp.float32),
            pltpu.VMEM(second.shape, bf),
            pltpu.VMEM(spread.shape, bf),
            pltpu.VMEM((stations, HALF * 2 * depth, frames // HALF * LANES), bf),
            pltpu.VMEM((frames // HALF, sc * groups, spread.shape[0]), bf),
            pltpu.VMEM((groups * sc, sc * groups), bf),
            pltpu.SemaphoreType.DMA((stations + 4,)),
        ],
        name="channelise",
    )(block_owner, volts, filter_taps, first, turn, second, spread)


def pieces(total, most):
    return max(d for d in range(1, most + 1) if total % d == 0)


def weights_kernel(pairs, weight_ref, copy_ref, out_ref, rows_ref):
    count, columns = weight_ref.shape
    tile, spread = copy_ref.shape
    frames = spread // tile

    @pl.when(pl.program_id(0) == 0)
    def _():
        for i in range(columns // tile):
            rows_ref[:, i * spread : (i + 1) * spread] = jnp.dot(
                weight_ref[:, i * tile : (i + 1) * tile], copy_ref[...], preferred_element_type=jnp.float32
            )

    width = out_ref.shape[1]
    owned = lax.broadcasted_iota(jnp.int32, (frames, width), 1) // pairs % frames == lax.broadcasted_iota(
        jnp.int32, (frames, width), 0
    )
    share = out_ref.shape[0] // frames

    def fill(i, carry):
        row = rows_ref[pl.ds(pl.program_id(0) * share + i, 1), :]
        out_ref[pl.ds(pl.multiple_of(i * frames, frames), frames), :] = jnp.where(
            owned, jnp.broadcast_to(row, (frames, width)), 0.0
        ).astype(jnp.bfloat16)
        return carry

    lax.fori_loop(0, share, fill, 0, unroll=pieces(share, 10))


def framed_weights(weights, frames, pairs):
    count, columns = weights.shape
    tile = min(LANES, columns)
    copies = np.einsum("bc,pq,f->bpcfq", np.eye(tile // pairs), np.eye(pairs), np.ones(frames)).reshape(tile, tile * frames)
    share = pieces(count, 100)
    return pl.pallas_call(
        functools.partial(weights_kernel, pairs),
        grid=(count // share,),
        out_shape=jax.ShapeDtypeStruct((count * frames, columns * frames), jnp.bfloat16),
        in_specs=[
            pl.BlockSpec((count, columns), lambda i: (0, 0)),
            pl.BlockSpec((tile, tile * frames), lambda i: (0, 0)),
        ],
        out_specs=pl.BlockSpec((share * frames, columns * frames), lambda i: (i, 0)),
        scratch_shapes=[pltpu.VMEM((count, columns * frames), jnp.float32)],
        name="framed_weights",
    )(weights, jnp.asarray(copies, jnp.bfloat16))


def correlate_kernel(owners, sections, frames, *refs):
    per = owners
    mine = refs[:per]
    twin_ref = refs[per]
    others = refs[per + 1 : per + 1 + per * (sections - 1)]
    out_ref, cross_ref, packed = refs[per + 1 + per * (sections - 1) :]
    rows, lanes = mine[0].shape
    pairs = rows // frames
    width = lanes // LANES
    block = owners * pairs
    here, section, pol = lax.axis_index("chan"), lax.axis_index("stat"), lax.axis_index("pol")
    f32 = jnp.float32

    def put(slot, k, ref, first):
        for j in range(width):
            for f in range(frames):
                packed[j, pl.ds(slot * block + k * pairs, pairs), pl.ds(f * LANES, LANES)] = ref[
                    pl.ds(first + f * pairs, pairs), pl.ds(j * LANES, LANES)
                ]

    for k in range(owners):
        put(0, k, mine[k], 0)
        put(1, k, twin_ref, k * rows)
        for x in range(1, sections):
            put(1 + x, k, others[(x - 1) * owners + k], 0)
    slots = 1 + sections
    products = []
    for j in range(width):
        x = packed[j]
        products.append(
            lax.dot_general(x[: 2 * block], x, (((1,), (1,)), ((), ())), preferred_element_type=f32)
        )
    members = block // 2
    inputs = out_ref.shape[1]
    col = lax.broadcasted_iota(jnp.int32, (slots * block, 1), 0)
    slot, inner = col // block, col % block
    k, station, part = inner // pairs, inner % pairs // 2, inner % 2
    there = jnp.where(slot == 1, 1 - pol, pol)
    source = section ^ jnp.where(slot > 1, slot - 1, 0)
    target = (source * 2 + there) * members + (here ^ k) * (pairs // 2) + station
    wide = lax.broadcasted_iota(jnp.int32, (slots * block, 2 * inputs), 1)
    pick = jnp.where(wide == target + part * inputs, 1.0, 0.0)
    pick_other = jnp.where(slot > 1, pick, 0.0)
    height = width * block
    left = lax.broadcasted_iota(jnp.int32, (height, height), 0)
    right = lax.broadcasted_iota(jnp.int32, (height, height), 1)
    inner = right % block
    k, station, part = inner // pairs, inner % pairs // 2, inner % 2
    aim = right // block * block + (here ^ k) * (pairs // 2) + station
    plain = jnp.where(left == aim + part * members, 1.0, 0.0)
    turned = jnp.where(left == aim + (1 - part) * members, jnp.where(part == 1, 1.0, -1.0), 0.0)
    factor = 1.0 / (frames * LANES)

    def settle(first, chosen):
        v = jnp.concatenate([p[first * block : (first + 1) * block] for p in products], 0)
        u = jnp.dot(v, chosen, preferred_element_type=f32, precision=lax.Precision.HIGHEST)
        total = jnp.dot(plain, u[:, :inputs], preferred_element_type=f32, precision=lax.Precision.HIGHEST)
        total += jnp.dot(turned, u[:, inputs:], preferred_element_type=f32, precision=lax.Precision.HIGHEST)
        return total * factor

    out_ref[...] = settle(0, pick)
    cross_ref[...] = settle(1, pick_other)


def correlate(mine, twin, others, frames, sections):
    owners = len(mine)
    rows, lanes = mine[0].shape
    width = lanes // LANES
    block = owners * rows // frames
    inputs = block // 2 * 2 * sections
    shape = jax.ShapeDtypeStruct((width * block, inputs), jnp.float32)
    vmem = pl.BlockSpec(memory_space=pltpu.VMEM)
    return pl.pallas_call(
        functools.partial(correlate_kernel, owners, sections, frames),
        out_shape=[shape, shape],
        in_specs=[vmem] * (len(mine) + 1 + len(others)),
        out_specs=[vmem, vmem],
        scratch_shapes=[pltpu.VMEM((width, (1 + sections) * block, frames * LANES), jnp.bfloat16)],
        name="correlate",
    )(*mine, twin, *others)


def beams_kernel(owners, sections, weight_ref, *refs):
    blocks, (out_ref, data) = refs[:-2], refs[-2:]
    rows = blocks[0].shape[0]
    here, section = lax.axis_index("chan"), lax.axis_index("stat")

    @pl.when(pl.program_id(0) == 0)
    def _():
        for x in range(sections):
            for k in range(owners):
                at = ((section ^ x) * owners + (here ^ k)) * rows
                data[pl.ds(pl.multiple_of(at, rows), rows), :] = blocks[x * owners + k][...]

    out_ref[...] = jnp.dot(weight_ref[...], data[...], preferred_element_type=jnp.float32)


def beamform(weights, blocks, owners, sections):
    height, depth = weights.shape
    rows, lanes = blocks[0].shape
    share = 8 * pieces(height // 8, max(1, 400 * 512 // depth // 8))
    whole = pl.BlockSpec((rows, lanes), lambda i: (0, 0))
    return pl.pallas_call(
        functools.partial(beams_kernel, owners, sections),
        grid=(height // share,),
        out_shape=jax.ShapeDtypeStruct((height, lanes), jnp.float32),
        in_specs=[pl.BlockSpec((share, depth), lambda i: (i, 0))] + [whole] * len(blocks),
        out_specs=pl.BlockSpec((share, lanes), lambda i: (i, 0)),
        scratch_shapes=[pltpu.VMEM((depth, lanes), jnp.bfloat16)],
        name="beamform",
    )(weights, *blocks)


def beam_weights(indices, beam_table, factor):
    levels = jnp.arange(beam_table.shape[1], dtype=jnp.int32)
    selected = indices[..., None] == levels
    real = jnp.sum(jnp.where(selected, beam_table[0], 0.0), axis=-1) * factor
    imag = jnp.sum(jnp.where(selected, beam_table[1], 0.0), axis=-1) * factor
    upper = jnp.stack([real, -imag], axis=-1)
    lower = jnp.stack([imag, real], axis=-1)
    return jnp.stack([upper, lower], axis=1).astype(jnp.bfloat16)


def partner(x, axis, distance):
    return lax.ppermute(x, axis, [(i, i ^ distance) for i in range(lax.axis_size(axis))])


def on_device(voltages, filter_taps, beam_table, beam_index, block_owner):
    owners, sections = lax.axis_size("chan"), lax.axis_size("stat")
    stations = voltages.shape[1]
    frames = voltages.shape[3] - filter_taps.shape[0] + 1
    pairs = 2 * stations
    groups = block_owner.shape[0]
    own = channelise(voltages, filter_taps, block_owner, owners)
    mine = [own[0]] + [partner(own[k], "chan", k) for k in range(1, owners)]
    lead = max(1, owners // 4)
    others = []
    for x in range(1, sections):
        for first in range(0, owners, lead):
            part = mine[first : first + lead]
            if lead == 1:
                others.append(partner(part[0], "stat", x))
            else:
                moved = partner(jnp.concatenate(part, 0), "stat", x)
                others.extend(jnp.split(moved, lead, 0))
    held = lax.optimization_barrier((jnp.concatenate(mine, 0), others[1]))[0]
    twin = partner(held, "pol", 1)

    beam_count, station_count = beam_index.shape
    owned = beam_count // sections
    index = lax.dynamic_slice_in_dim(beam_index, lax.axis_index("stat") * owned, owned, 0)
    weights = beam_weights(index, beam_table, 1.0 / math.sqrt(station_count)).reshape(2 * owned, 2 * station_count)
    weights = framed_weights(weights, frames, pairs)

    vis, cross = correlate(mine, twin, others, frames, sections)
    crossed = partner(cross, "pol", 1)
    last, _ = lax.optimization_barrier((others[-1], cross))
    beams = beamform(weights, mine + others[:-1] + [last], owners, sections)
    vis = (vis + crossed).reshape(groups // owners, 2, -1, vis.shape[1])
    return vis, beams.reshape(owned, 1, 2, frames, -1)


def solution(mesh):
    return jax.shard_map(
        on_device,
        mesh=mesh,
        in_specs=(P(("group", "stat"), "chan", "pol", None, None, None), P(), P(), P(), P()),
        out_specs=(
            P(("group", "chan"), None, ("stat", "pol"), None),
            P(("group", "stat"), "pol", None, None, "chan"),
        ),
        check_vma=False,
    )
```

```python
import functools, math
import jax, jax.numpy as jnp, numpy as np
from jax import lax
from jax.experimental import pallas as pl
from jax.experimental.pallas import tpu as pltpu
from jax.sharding import PartitionSpec as P


LANES = 128
HALF = 4


def dft_parts(rows, cols, length):
    phase = np.outer(np.arange(rows), np.arange(cols)) % length * (2.0 * np.pi / length)
    return np.cos(phase), np.sin(phase)


def channel_tables(nfft, groups):
    depth = nfft // LANES
    per_group = LANES // depth
    cosine, sine = dft_parts(depth, depth, depth)
    pair = np.stack([np.stack([cosine, sine], -1), np.stack([-sine, cosine], -1)])
    first = np.einsum("akrc,fg->afkgrc", pair, np.eye(HALF))
    first = first.reshape(2 * HALF * depth, HALF * depth * 2)
    turn_cos, turn_sin = dft_parts(depth, LANES, nfft)
    cosine, sine = dft_parts(LANES, LANES, LANES)
    order = (np.arange(groups)[None, :] * per_group + np.arange(per_group)[:, None]).reshape(-1)
    cosine, sine = cosine[order] / math.sqrt(nfft), sine[order] / math.sqrt(nfft)
    second = np.concatenate([np.concatenate([cosine, sine], 1), np.concatenate([-sine, cosine], 1)], 0)
    spread = np.einsum("qr,fg,kl->qfkgrl", np.eye(per_group), np.eye(HALF), np.eye(depth))
    spread = spread.reshape(per_group * HALF * depth, HALF * per_group * depth)
    bf = lambda x: jnp.asarray(x, jnp.bfloat16)
    return bf(first), jnp.asarray(np.stack([turn_cos, turn_sin]), jnp.float32), bf(second), bf(spread)


def channel_kernel(owners, owner_ref, volt_ref, taps_ref, first_ref, turn_ref, second_ref, spread_ref, *rest):
    outs = rest[:owners]
    volts, tap_rows, first, turn, second, spread, filt, wide, pick, sems = rest[owners:]
    stations, blocks, rows, _ = volt_ref.shape
    taps = taps_ref.shape[0]
    frames = blocks - taps + 1
    halves = frames // HALF
    depth = rows // 2
    groups = owner_ref.shape[0]
    width = groups // owners
    quads = LANES // depth
    span = HALF * depth
    here = lax.axis_index("chan")
    copies = []
    for s in range(stations):
        copies.append(pltpu.make_async_copy(volt_ref.at[s], volts.at[s], sems.at[s]))
    consts = []
    for i, (src, dst) in enumerate([(first_ref, first), (turn_ref, turn), (second_ref, second), (spread_ref, spread)]):
        consts.append(pltpu.make_async_copy(src, dst, sems.at[stations + i]))
    for c in copies + consts:
        c.start()

    sub = lax.broadcasted_iota(jnp.int32, (8, LANES), 0)
    for t in range(taps):
        for m in range(rows // 8):
            parts = [jnp.broadcast_to(taps_ref[t : t + 1, pl.ds((4 * m + i) * LANES, LANES)], (8, LANES)) for i in range(4)]
            low = jnp.where(sub < 2, parts[0], parts[1])
            high = jnp.where(sub < 6, parts[2], parts[3])
            tap_rows[t, pl.ds(8 * m, 8), :] = jnp.where(sub < 4, low, high)

    sc = 2 * stations
    lane = lax.broadcasted_iota(jnp.int32, (sc, sc * groups), 1)
    base = lax.broadcasted_iota(jnp.int32, (sc, sc * groups), 0) * groups
    for k in range(owners):
        for j in range(width):
            g = owner_ref[(here ^ k) * width + j]
            p = (k * width + j) * sc
            pick[pl.ds(p, sc), :] = jnp.where(lane == base + g, 1.0, 0.0).astype(jnp.bfloat16)

    step = 16
    for s in range(stations):
        copies[s].wait()

        def fir(m, carry, s=s):
            at = pl.multiple_of(m * step, step)
            x = [volts[s, b, pl.ds(at, step), :].astype(jnp.float32) for b in range(blocks)]
            w = [tap_rows[t, pl.ds(at, step), :] for t in range(taps)]
            for f in range(frames):
                total = w[0] * x[f]
                for t in range(1, taps):
                    total = total + w[t] * x[f + t]
                row = pl.multiple_of((f % HALF) * rows + at, step)
                filt[s, pl.ds(row, step), pl.ds((f // HALF) * LANES, LANES)] = total.astype(jnp.bfloat16)
            return carry

        lax.fori_loop(0, rows // step, fir, 0)

    for c in consts:
        c.wait()
    f32 = jnp.float32
    cosine = jnp.concatenate([turn[0]] * HALF, 0)
    sine = jnp.concatenate([turn[1]] * HALF, 0)
    for s in range(stations):
        y = jnp.dot(first[...], filt[s], preferred_element_type=f32)
        re, im = y[:span], y[span:]
        turned = []
        for h in range(halves):
            a, b = re[:, h * LANES : (h + 1) * LANES], im[:, h * LANES : (h + 1) * LANES]
            turned.append(jnp.concatenate([a * cosine + b * sine, b * cosine - a * sine], 1))
        turned = jnp.concatenate(turned, 0).astype(jnp.bfloat16)
        z = lax.dot_general(second[...], turned, (((1,), (1,)), ((), ())), preferred_element_type=f32).astype(jnp.bfloat16)
        for c in range(2):
            for q in range(quads):
                for h in range(halves):
                    wide[h, pl.ds((s * 2 + c) * groups, groups), pl.ds(q * LANES, LANES)] = z[
                        c * quads * groups + q * groups : c * quads * groups + (q + 1) * groups, h * LANES : (h + 1) * LANES
                    ]
    for h in range(halves):
        y = jnp.dot(wide[h], spread[...], preferred_element_type=f32).astype(jnp.bfloat16)
        z = jnp.dot(pick[...], y, preferred_element_type=f32)
        for k in range(owners):
            for j in range(width):
                for f in range(HALF):
                    p = (k * width + j) * sc
                    outs[k][pl.ds((h * HALF + f) * sc, sc), pl.ds(j * LANES, LANES)] = z[
                        p : p + sc, f * LANES : (f + 1) * LANES
                    ].astype(jnp.bfloat16)


def channelise(voltages, filter_taps, block_owner, owners):
    _, stations, _, blocks, _, nfft = voltages.shape
    taps = filter_taps.shape[0]
    frames = blocks - taps + 1
    groups = block_owner.shape[0]
    depth = nfft // LANES
    volts = voltages.reshape(stations, blocks, 2, depth, LANES).transpose(0, 1, 3, 2, 4).reshape(stations, blocks, 2 * depth, LANES)
    first, turn, second, spread = channel_tables(nfft, groups)
    sc = 2 * stations
    width = groups // owners
    anyspec = pl.BlockSpec(memory_space=pl.ANY)
    bf = jnp.bfloat16
    return pl.pallas_call(
        functools.partial(channel_kernel, owners),
        out_shape=[jax.ShapeDtypeStruct((frames * sc, width * LANES), bf)] * owners,
        in_specs=[pl.BlockSpec(memory_space=pltpu.SMEM), anyspec, pl.BlockSpec(memory_space=pltpu.VMEM)] + [anyspec] * 4,
        out_specs=[pl.BlockSpec(memory_space=pltpu.VMEM)] * owners,
        scratch_shapes=[
            pltpu.VMEM(volts.shape, bf),
            pltpu.VMEM((taps, 2 * depth, LANES), jnp.float32),
            pltpu.VMEM(first.shape, bf),
            pltpu.VMEM(turn.shape, jnp.float32),
            pltpu.VMEM(second.shape, bf),
            pltpu.VMEM(spread.shape, bf),
            pltpu.VMEM((stations, HALF * 2 * depth, frames // HALF * LANES), bf),
            pltpu.VMEM((frames // HALF, sc * groups, spread.shape[0]), bf),
            pltpu.VMEM((groups * sc, sc * groups), bf),
            pltpu.SemaphoreType.DMA((stations + 4,)),
        ],
        compiler_params=grant(),
        name="channelise",
    )(block_owner, volts, filter_taps, first, turn, second, spread)


VMEM_BYTES = 24 * 2**20
RESIDENT = 8 * 2**20
SLICE = 32


def whole_vmem(count):
    return [pl.BlockSpec(memory_space=pltpu.VMEM)] * count


def grant(size=VMEM_BYTES):
    return pltpu.CompilerParams(vmem_limit_bytes=size)


def pieces(total, most):
    return max(d for d in range(1, most + 1) if total % d == 0)


def split_low(x, size):
    shift = size.bit_length() - 1
    assert size == 1 << shift
    return x >> shift, x & (size - 1)


def bf_pair(x):
    high = x.astype(jnp.bfloat16)
    return high, (x - high.astype(jnp.float32)).astype(jnp.bfloat16)


def dot_tt(a, b):
    return lax.dot_general(a, b, (((1,), (1,)), ((), ())), preferred_element_type=jnp.float32)


def weights_kernel(pairs, owned, share, table_ref, index_ref, copy_ref, out_ref, rows_ref):
    stations, beams = index_ref.shape
    tile, spread = copy_ref.shape
    frames = spread // tile
    count = 2 * owned
    start = lax.axis_index("stat") * owned
    factor = 1.0 / math.sqrt(stations)

    def prepare():
        row = lax.broadcasted_iota(jnp.int32, (count, beams), 0)
        lane = lax.broadcasted_iota(jnp.int32, (count, beams), 1)
        hit = lane == start + (row >> 1)
        one, zero = jnp.float32(1), jnp.float32(0)
        choose = [jnp.where(hit & ((row & 1) == c), one, zero).astype(jnp.bfloat16) for c in range(2)]
        for i in range(stations // SLICE):
            index = index_ref[i * SLICE : (i + 1) * SLICE, :]
            real = jnp.zeros(index.shape, jnp.float32)
            imag = jnp.zeros(index.shape, jnp.float32)
            for e in range(table_ref.shape[1]):
                here = index == e
                real = jnp.where(here, table_ref[0, e], real)
                imag = jnp.where(here, table_ref[1, e], imag)
            real, imag = real * factor, imag * factor
            upper = jnp.concatenate([real, -imag], 0).astype(jnp.bfloat16)
            lower = jnp.concatenate([imag, real], 0).astype(jnp.bfloat16)
            w = dot_tt(choose[0], upper) + dot_tt(choose[1], lower)
            rows_ref[:, i * spread : (i + 1) * spread] = jnp.dot(
                w.astype(jnp.bfloat16), copy_ref[...], preferred_element_type=jnp.float32
            )

    first = 0
    if share == count:
        prepare()
    else:
        pl.when(pl.program_id(0) == 0)(prepare)
        first = pl.program_id(0) * share
    width = out_ref.shape[1]
    lane = lax.broadcasted_iota(jnp.int32, (frames, width), 1)
    mine = split_low(split_low(lane, pairs)[0], frames)[1] == lax.broadcasted_iota(jnp.int32, (frames, width), 0)

    def fill(i, carry):
        row = rows_ref[pl.ds(first + i, 1), :]
        out_ref[pl.ds(pl.multiple_of(i * frames, frames), frames), :] = jnp.where(
            mine, jnp.broadcast_to(row, (frames, width)), 0.0
        ).astype(jnp.bfloat16)
        return carry

    lax.fori_loop(0, share, fill, 0, unroll=pieces(share, 10))


def framed_weights(beam_table, beam_index, frames, pairs, owned):
    stations = beam_index.shape[1]
    eye = np.eye
    copies = np.einsum("bp,sq,ct,f->cbspqft", eye(2 * SLICE // pairs), eye(pairs // 2), eye(2), np.ones(frames))
    copies = np.moveaxis(copies, (3, 5, 4, 6), (3, 4, 5, 6)).reshape(2 * SLICE, 2 * SLICE * frames)
    depth = 2 * stations * frames
    count = 2 * owned
    resident = count * frames * depth * 2 <= RESIDENT
    share = count if resident else pieces(count, 10)
    smem = pl.BlockSpec(memory_space=pltpu.SMEM)
    inputs = (beam_table, beam_index.T, jnp.asarray(copies, jnp.bfloat16))
    extra = {}
    if not resident:
        extra = dict(grid=(count // share,), out_specs=pl.BlockSpec((share * frames, depth), lambda i: (i, 0)))
    return pl.pallas_call(
        functools.partial(weights_kernel, pairs, owned, share),
        out_shape=jax.ShapeDtypeStruct((count * frames, depth), jnp.bfloat16),
        in_specs=[smem] + whole_vmem(2),
        scratch_shapes=[pltpu.VMEM((count, depth), jnp.float32)],
        compiler_params=grant() if resident else None,
        name="framed_weights",
        **extra,
    )(*inputs)


def pack(packed, slot, blocks, frames):
    rows, lanes = blocks[0].shape
    pairs = rows // frames
    for k, ref in enumerate(blocks):
        at = (slot * len(blocks) + k) * pairs
        for j in range(lanes // LANES):
            for f in range(frames):
                packed[j, pl.ds(at, pairs), pl.ds(f * LANES, LANES)] = ref[
                    pl.ds(f * pairs, pairs), pl.ds(j * LANES, LANES)
                ]


def settle(products, spread, merge):
    inputs = spread.shape[1] // 2
    v = bf_pair(jnp.concatenate(products, 0))
    u = sum(jnp.dot(x, spread, preferred_element_type=jnp.float32) for x in v)
    u = bf_pair(jnp.concatenate([u[:, :inputs], u[:, inputs:]], 0))
    return sum(jnp.dot(merge, x, preferred_element_type=jnp.float32) for x in u)


def near_kernel(owners, sections, frames, *refs):
    mine, twin = refs[:owners], refs[owners : 2 * owners]
    part_ref, packed, merge_ref, far_ref = refs[2 * owners :]
    width = packed.shape[0]
    pairs = mine[0].shape[0] // frames
    block = owners * pairs
    members = block // 2
    inputs = part_ref.shape[1]
    here, section, pol = lax.axis_index("chan"), lax.axis_index("stat"), lax.axis_index("pol")
    pack(packed, 0, mine, frames)
    pack(packed, 1, twin, frames)
    one, zero = jnp.float32(1), jnp.float32(0)

    def spread_of(slots, source, there):
        col = lax.broadcasted_iota(jnp.int32, (slots * block, 1), 0)
        slot, inner = split_low(col, block)
        k, rest = split_low(inner, pairs)
        target = (source(slot) * 2 + there(slot)) * members + (here ^ k) * (pairs // 2) + (rest >> 1)
        wide = lax.broadcasted_iota(jnp.int32, (slots * block, 2 * inputs), 1)
        return jnp.where(wide == target + (rest & 1) * inputs, one, zero).astype(jnp.bfloat16)

    near = spread_of(2, lambda slot: section, lambda slot: pol ^ slot)
    far_ref[...] = spread_of(sections - 1, lambda slot: section ^ (slot + 1), lambda slot: pol)
    height = width * block
    left = lax.broadcasted_iota(jnp.int32, (height, height), 0)
    right = lax.broadcasted_iota(jnp.int32, (1, height), 1)
    j, inner = split_low(right, block)
    k, rest = split_low(inner, pairs)
    aim = j * block + (here ^ k) * (pairs // 2) + (rest >> 1)
    part = rest & 1
    scale = jnp.float32(1)
    merge_ref[:, :height] = jnp.where(left == aim + part * members, scale, zero).astype(jnp.bfloat16)
    sign = jnp.where(part == 1, scale, -scale)
    merge_ref[:, height:] = jnp.where(left == aim + (1 - part) * members, sign, zero).astype(jnp.bfloat16)
    products = [dot_tt(packed[j, :block], packed[j]) for j in range(width)]
    part_ref[...] = settle(products, near, merge_ref[...]) * (1.0 / (frames * LANES))


def far_kernel(owners, sections, frames, part_ref, packed, merge_ref, far_ref, *refs):
    others = refs[: owners * (sections - 1)]
    out_ref, cross_ref, theirs = refs[owners * (sections - 1) :]
    width, double, _ = packed.shape
    block = double // 2
    for x in range(sections - 1):
        pack(theirs, x, others[x * owners : (x + 1) * owners], frames)
    products = [dot_tt(packed[j], theirs[j]) for j in range(width)]
    factor = 1.0 / (frames * LANES)
    out_ref[...] = part_ref[...] + settle([p[:block] for p in products], far_ref[...], merge_ref[...]) * factor
    cross_ref[...] = settle([p[block:] for p in products], far_ref[...], merge_ref[...]) * factor


def correlate_near(mine, twin, frames, sections):
    owners = len(mine)
    rows, lanes = mine[0].shape
    width, block = lanes // LANES, owners * rows // frames
    inputs = block * sections
    bf = jnp.bfloat16
    return pl.pallas_call(
        functools.partial(near_kernel, owners, sections, frames),
        out_shape=[
            jax.ShapeDtypeStruct((width * block, inputs), jnp.float32),
            jax.ShapeDtypeStruct((width, 2 * block, frames * LANES), bf),
            jax.ShapeDtypeStruct((width * block, 2 * width * block), bf),
            jax.ShapeDtypeStruct(((sections - 1) * block, 2 * inputs), bf),
        ],
        in_specs=whole_vmem(2 * owners),
        out_specs=whole_vmem(4),
        compiler_params=grant(),
        name="correlate_near",
    )(*mine, *twin)


def correlate_far(near, others, owners, frames, sections):
    part, packed, merge, far = near
    shape = jax.ShapeDtypeStruct(part.shape, jnp.float32)
    width, double, lanes = packed.shape
    return pl.pallas_call(
        functools.partial(far_kernel, owners, sections, frames),
        out_shape=[shape, shape],
        in_specs=whole_vmem(4 + len(others)),
        out_specs=whole_vmem(2),
        scratch_shapes=[pltpu.VMEM((width, (sections - 1) * double // 2, lanes), jnp.bfloat16)],
        compiler_params=grant(),
        name="correlate_far",
    )(part, packed, merge, far, *others)


def gather_rows(data, blocks, owners, sections):
    rows = blocks[0].shape[0]
    here, section = lax.axis_index("chan"), lax.axis_index("stat")
    for x in range(sections):
        for k in range(owners):
            at = ((section ^ x) * owners + (here ^ k)) * rows
            data[pl.ds(pl.multiple_of(at, rows), rows), :] = blocks[x * owners + k][...]


def beams_resident(owners, sections, share, span, weight_ref, *refs):
    blocks, (out_ref, data, held, sems) = refs[:-4], refs[-4:]
    gather_rows(data, blocks, owners, sections)
    slots = held.shape[0]
    steps = []
    for row in range(0, weight_ref.shape[0], share):
        for lane in range(0, data.shape[1], span):
            steps.append((row, lane))

    def copy(i):
        row, lane = steps[i]
        return pltpu.make_async_copy(
            held.at[i % slots], out_ref.at[pl.ds(row, share), pl.ds(lane, span)], sems.at[i % slots]
        )

    for i, (row, lane) in enumerate(steps):
        if i >= slots:
            copy(i - slots).wait()
        held[i % slots] = jnp.dot(
            weight_ref[row : row + share, :], data[:, lane : lane + span], preferred_element_type=jnp.float32
        )
        copy(i).start()
    for i in range(max(0, len(steps) - slots), len(steps)):
        copy(i).wait()


def beams_streamed(owners, sections, weight_ref, *refs):
    blocks, (out_ref, data) = refs[:-2], refs[-2:]
    pl.when(pl.program_id(0) == 0)(lambda: gather_rows(data, blocks, owners, sections))
    out_ref[...] = jnp.dot(weight_ref[...], data[...], preferred_element_type=jnp.float32)


def beamform(weights, blocks, owners, sections):
    height, depth = weights.shape
    rows, lanes = blocks[0].shape
    shape = jax.ShapeDtypeStruct((height, lanes), jnp.float32)
    data = pltpu.VMEM((depth, lanes), jnp.bfloat16)
    if height * depth * 2 <= RESIDENT:
        span = min(lanes, 512)
        share = 8 * pieces(height // 8, 100)
        slots = 4
        return pl.pallas_call(
            functools.partial(beams_resident, owners, sections, share, span),
            out_shape=shape,
            in_specs=whole_vmem(1 + len(blocks)),
            out_specs=pl.BlockSpec(memory_space=pl.ANY),
            scratch_shapes=[data, pltpu.VMEM((slots, share, span), jnp.float32), pltpu.SemaphoreType.DMA((slots,))],
            compiler_params=grant(),
            name="beamform",
        )(weights, *blocks)
    share = 8 * pieces(height // 8, max(1, 400 * 512 // depth // 8))
    whole = pl.BlockSpec((rows, lanes), lambda i: (0, 0))
    return pl.pallas_call(
        functools.partial(beams_streamed, owners, sections),
        grid=(height // share,),
        out_shape=shape,
        in_specs=[pl.BlockSpec((share, depth), lambda i: (i, 0))] + [whole] * len(blocks),
        out_specs=pl.BlockSpec((share, lanes), lambda i: (i, 0)),
        scratch_shapes=[data],
        name="beamform",
    )(weights, *blocks)


def partner(x, axis, distance):
    return lax.ppermute(x, axis, [(i, i ^ distance) for i in range(lax.axis_size(axis))])


def moved(parts, axis, distance):
    if len(parts) == 1:
        return [partner(parts[0], axis, distance)]
    return jnp.split(partner(jnp.concatenate(parts, 0), axis, distance), len(parts), 0)


def on_device(voltages, filter_taps, beam_table, beam_index, block_owner):
    owners, sections = lax.axis_size("chan"), lax.axis_size("stat")
    stations = voltages.shape[1]
    frames = voltages.shape[3] - filter_taps.shape[0] + 1
    pairs = 2 * stations
    groups = block_owner.shape[0]
    owned = beam_index.shape[0] // sections
    own = channelise(voltages, filter_taps, block_owner, owners)
    weights = framed_weights(beam_table, beam_index, frames, pairs, owned)
    mine = [own[0]] + [partner(own[k], "chan", k) for k in range(1, owners)]
    lead = max(1, owners // 4)
    twin, others = [], [[] for _ in range(1, sections)]
    for g in range(owners // lead):
        part = mine[g * lead : (g + 1) * lead]
        for x in range(1, sections):
            others[x - 1] += moved(part, "stat", x)
        twin += moved(part, "pol", 1)
    others = sum(others, [])
    near = correlate_near(mine, twin, frames, sections)
    vis, cross = correlate_far(near, others, owners, frames, sections)
    crossed = partner(cross, "pol", 1)
    last, _ = lax.optimization_barrier((others[-1], cross))
    beams = beamform(weights, mine + others[:-1] + [last], owners, sections)
    vis = (vis + crossed).reshape(groups // owners, 2, -1, vis.shape[1])
    return vis, beams.reshape(owned, 1, 2, frames, -1)


def solution(mesh):
    return jax.shard_map(
        on_device,
        mesh=mesh,
        in_specs=(P(("group", "stat"), "chan", "pol", None, None, None), P(), P(), P(), P()),
        out_specs=(
            P(("group", "chan"), None, ("stat", "pol"), None),
            P(("group", "stat"), "pol", None, None, "chan"),
        ),
        check_vma=False,
    )
```

```python
import functools, math
import jax, jax.numpy as jnp, numpy as np
from jax import lax
from jax.experimental import pallas as pl
from jax.experimental.pallas import tpu as pltpu
from jax.sharding import PartitionSpec as P


LANES = 128
HALF = 4


def dft_parts(rows, cols, length):
    phase = np.outer(np.arange(rows), np.arange(cols)) % length * (2.0 * np.pi / length)
    return np.cos(phase), np.sin(phase)


def channel_tables(nfft, groups):
    depth = nfft // LANES
    per_group = LANES // depth
    cosine, sine = dft_parts(depth, depth, depth)
    pair = np.stack([np.stack([cosine, sine], -1), np.stack([-sine, cosine], -1)])
    first = np.einsum("akrc,fg->afkgrc", pair, np.eye(HALF))
    first = first.reshape(2 * HALF * depth, HALF * depth * 2)
    turn_cos, turn_sin = dft_parts(depth, LANES, nfft)
    cosine, sine = dft_parts(LANES, LANES, LANES)
    order = (np.arange(groups)[None, :] * per_group + np.arange(per_group)[:, None]).reshape(-1)
    cosine, sine = cosine[order] / math.sqrt(nfft), sine[order] / math.sqrt(nfft)
    second = np.concatenate([np.concatenate([cosine, sine], 1), np.concatenate([-sine, cosine], 1)], 0)
    spread = np.einsum("qr,fg,kl->qfkgrl", np.eye(per_group), np.eye(HALF), np.eye(depth))
    spread = spread.reshape(per_group * HALF * depth, HALF * per_group * depth)
    bf = lambda x: jnp.asarray(x, jnp.bfloat16)
    return bf(first), jnp.asarray(np.stack([turn_cos, turn_sin]), jnp.float32), bf(second), bf(spread)


def channel_kernel(owners, owner_ref, volt_ref, taps_hbm, first_ref, turn_ref, second_ref, spread_ref, *rest):
    outs = rest[:owners]
    volts, taps_ref, tap_rows, first, turn, second, spread, filt, wide, pick, sems = rest[owners:]
    stations, blocks, rows, _ = volt_ref.shape
    taps = taps_ref.shape[0]
    frames = blocks - taps + 1
    halves = frames // HALF
    depth = rows // 2
    groups = owner_ref.shape[0]
    width = groups // owners
    quads = LANES // depth
    span = HALF * depth
    here = lax.axis_index("chan")
    tap_copy = pltpu.make_async_copy(taps_hbm, taps_ref, sems.at[stations + 4])
    tap_copy.start()
    copies = []
    for s in range(stations):
        copies.append(pltpu.make_async_copy(volt_ref.at[s], volts.at[s], sems.at[s]))
    consts = []
    for i, (src, dst) in enumerate([(first_ref, first), (turn_ref, turn), (second_ref, second), (spread_ref, spread)]):
        consts.append(pltpu.make_async_copy(src, dst, sems.at[stations + i]))
    for c in copies + consts:
        c.start()
    tap_copy.wait()

    sub = lax.broadcasted_iota(jnp.int32, (8, LANES), 0)
    for t in range(taps):
        for m in range(rows // 8):
            parts = [jnp.broadcast_to(taps_ref[t : t + 1, pl.ds((4 * m + i) * LANES, LANES)], (8, LANES)) for i in range(4)]
            low = jnp.where(sub < 2, parts[0], parts[1])
            high = jnp.where(sub < 6, parts[2], parts[3])
            tap_rows[t, pl.ds(8 * m, 8), :] = jnp.where(sub < 4, low, high)

    sc = 2 * stations
    lane = lax.broadcasted_iota(jnp.int32, (sc, sc * groups), 1)
    base = lax.broadcasted_iota(jnp.int32, (sc, sc * groups), 0) * groups
    for k in range(owners):
        for j in range(width):
            g = owner_ref[(here ^ k) * width + j]
            p = (k * width + j) * sc
            pick[pl.ds(p, sc), :] = jnp.where(lane == base + g, 1.0, 0.0).astype(jnp.bfloat16)

    step = 16
    for s in range(stations):
        copies[s].wait()

        def fir(m, carry, s=s):
            at = pl.multiple_of(m * step, step)
            x = [volts[s, b, pl.ds(at, step), :].astype(jnp.float32) for b in range(blocks)]
            w = [tap_rows[t, pl.ds(at, step), :] for t in range(taps)]
            for f in range(frames):
                total = w[0] * x[f]
                for t in range(1, taps):
                    total = total + w[t] * x[f + t]
                row = pl.multiple_of((f % HALF) * rows + at, step)
                filt[s, pl.ds(row, step), pl.ds((f // HALF) * LANES, LANES)] = total.astype(jnp.bfloat16)
            return carry

        lax.fori_loop(0, rows // step, fir, 0)

    for c in consts:
        c.wait()
    f32 = jnp.float32
    cosine = jnp.concatenate([turn[0]] * HALF, 0)
    sine = jnp.concatenate([turn[1]] * HALF, 0)
    for s in range(stations):
        y = jnp.dot(first[...], filt[s], preferred_element_type=f32)
        re, im = y[:span], y[span:]
        turned = []
        for h in range(halves):
            a, b = re[:, h * LANES : (h + 1) * LANES], im[:, h * LANES : (h + 1) * LANES]
            turned.append(jnp.concatenate([a * cosine + b * sine, b * cosine - a * sine], 1))
        turned = jnp.concatenate(turned, 0).astype(jnp.bfloat16)
        z = lax.dot_general(second[...], turned, (((1,), (1,)), ((), ())), preferred_element_type=f32).astype(jnp.bfloat16)
        for c in range(2):
            for q in range(quads):
                for h in range(halves):
                    wide[h, pl.ds((s * 2 + c) * groups, groups), pl.ds(q * LANES, LANES)] = z[
                        c * quads * groups + q * groups : c * quads * groups + (q + 1) * groups, h * LANES : (h + 1) * LANES
                    ]
    for h in range(halves):
        y = jnp.dot(wide[h], spread[...], preferred_element_type=f32).astype(jnp.bfloat16)
        z = jnp.dot(pick[...], y, preferred_element_type=f32)
        for k in range(owners):
            for j in range(width):
                for f in range(HALF):
                    p = (k * width + j) * sc
                    outs[k][pl.ds((h * HALF + f) * sc, sc), pl.ds(j * LANES, LANES)] = z[
                        p : p + sc, f * LANES : (f + 1) * LANES
                    ].astype(jnp.bfloat16)


def channelise(voltages, filter_taps, block_owner, owners):
    _, stations, _, blocks, _, nfft = voltages.shape
    taps = filter_taps.shape[0]
    frames = blocks - taps + 1
    groups = block_owner.shape[0]
    depth = nfft // LANES
    volts = voltages.reshape(stations, blocks, 2, depth, LANES).transpose(0, 1, 3, 2, 4).reshape(stations, blocks, 2 * depth, LANES)
    first, turn, second, spread = channel_tables(nfft, groups)
    sc = 2 * stations
    width = groups // owners
    anyspec = pl.BlockSpec(memory_space=pltpu.HBM)
    bf = jnp.bfloat16
    return pl.pallas_call(
        functools.partial(channel_kernel, owners),
        out_shape=[jax.ShapeDtypeStruct((frames * sc, width * LANES), bf)] * owners,
        in_specs=[pl.BlockSpec(memory_space=pltpu.SMEM)] + [anyspec] * 6,
        out_specs=[pl.BlockSpec(memory_space=pltpu.VMEM)] * owners,
        scratch_shapes=[
            pltpu.VMEM(volts.shape, bf),
            pltpu.VMEM(filter_taps.shape, jnp.float32),
            pltpu.VMEM((taps, 2 * depth, LANES), jnp.float32),
            pltpu.VMEM(first.shape, bf),
            pltpu.VMEM(turn.shape, jnp.float32),
            pltpu.VMEM(second.shape, bf),
            pltpu.VMEM(spread.shape, bf),
            pltpu.VMEM((stations, HALF * 2 * depth, frames // HALF * LANES), bf),
            pltpu.VMEM((frames // HALF, sc * groups, spread.shape[0]), bf),
            pltpu.VMEM((groups * sc, sc * groups), bf),
            pltpu.SemaphoreType.DMA((stations + 5,)),
        ],
        name="channelise",
    )(block_owner, volts, filter_taps, first, turn, second, spread)


VMEM_BYTES = 24 * 2**20
RESIDENT = 8 * 2**20
SLICE = 32


def whole_vmem(count):
    return [pl.BlockSpec(memory_space=pltpu.VMEM)] * count


def grant(size=VMEM_BYTES):
    return pltpu.CompilerParams(vmem_limit_bytes=size)


def pieces(total, most):
    return max(d for d in range(1, most + 1) if total % d == 0)


def split_low(x, size):
    shift = size.bit_length() - 1
    assert size == 1 << shift
    return x >> shift, x & (size - 1)


def bf_pair(x):
    high = x.astype(jnp.bfloat16)
    return high, (x - high.astype(jnp.float32)).astype(jnp.bfloat16)


def dot_tt(a, b):
    return lax.dot_general(a, b, (((1,), (1,)), ((), ())), preferred_element_type=jnp.float32)


def weights_kernel(pairs, owned, share, table_ref, index_hbm, copy_hbm, out_ref, rows_ref, index_ref, copy_ref, sems):
    stations, beams = index_ref.shape
    tile, spread = copy_ref.shape
    frames = spread // tile
    count = 2 * owned
    start = lax.axis_index("stat") * owned
    factor = 1.0 / math.sqrt(stations)

    def prepare():
        loads = [
            pltpu.make_async_copy(index_hbm, index_ref, sems.at[0]),
            pltpu.make_async_copy(copy_hbm, copy_ref, sems.at[1]),
        ]
        for load in loads:
            load.start()
        for load in loads:
            load.wait()
        row = lax.broadcasted_iota(jnp.int32, (count, beams), 0)
        lane = lax.broadcasted_iota(jnp.int32, (count, beams), 1)
        hit = lane == start + (row >> 1)
        one, zero = jnp.float32(1), jnp.float32(0)
        choose = [jnp.where(hit & ((row & 1) == c), one, zero).astype(jnp.bfloat16) for c in range(2)]
        for i in range(stations // SLICE):
            index = index_ref[i * SLICE : (i + 1) * SLICE, :]
            real = jnp.zeros(index.shape, jnp.float32)
            imag = jnp.zeros(index.shape, jnp.float32)
            for e in range(table_ref.shape[1]):
                here = index == e
                real = jnp.where(here, table_ref[0, e], real)
                imag = jnp.where(here, table_ref[1, e], imag)
            real, imag = real * factor, imag * factor
            upper = jnp.concatenate([real, -imag], 0).astype(jnp.bfloat16)
            lower = jnp.concatenate([imag, real], 0).astype(jnp.bfloat16)
            w = dot_tt(choose[0], upper) + dot_tt(choose[1], lower)
            rows_ref[:, i * spread : (i + 1) * spread] = jnp.dot(
                w.astype(jnp.bfloat16), copy_ref[...], preferred_element_type=jnp.float32
            )

    first = 0
    if share == count:
        prepare()
    else:
        pl.when(pl.program_id(0) == 0)(prepare)
        first = pl.program_id(0) * share
    width = out_ref.shape[1]
    lane = lax.broadcasted_iota(jnp.int32, (frames, width), 1)
    mine = split_low(split_low(lane, pairs)[0], frames)[1] == lax.broadcasted_iota(jnp.int32, (frames, width), 0)

    def fill(i, carry):
        row = rows_ref[pl.ds(first + i, 1), :]
        out_ref[pl.ds(pl.multiple_of(i * frames, frames), frames), :] = jnp.where(
            mine, jnp.broadcast_to(row, (frames, width)), 0.0
        ).astype(jnp.bfloat16)
        return carry

    lax.fori_loop(0, share, fill, 0, unroll=pieces(share, 10))


def framed_weights(beam_table, beam_index, frames, pairs, owned):
    stations = beam_index.shape[1]
    eye = np.eye
    copies = np.einsum("bp,sq,ct,f->cbspqft", eye(2 * SLICE // pairs), eye(pairs // 2), eye(2), np.ones(frames))
    copies = np.moveaxis(copies, (3, 5, 4, 6), (3, 4, 5, 6)).reshape(2 * SLICE, 2 * SLICE * frames)
    depth = 2 * stations * frames
    count = 2 * owned
    resident = count * frames * depth * 2 <= RESIDENT
    share = count if resident else pieces(count, 10)
    smem = pl.BlockSpec(memory_space=pltpu.SMEM)
    inputs = (beam_table, beam_index.T, jnp.asarray(copies, jnp.bfloat16))
    extra = {}
    if not resident:
        extra = dict(grid=(count // share,), out_specs=pl.BlockSpec((share * frames, depth), lambda i: (i, 0)))
    return pl.pallas_call(
        functools.partial(weights_kernel, pairs, owned, share),
        out_shape=jax.ShapeDtypeStruct((count * frames, depth), jnp.bfloat16),
        in_specs=[smem] + [pl.BlockSpec(memory_space=pltpu.HBM)] * 2,
        scratch_shapes=[
            pltpu.VMEM((count, depth), jnp.float32),
            pltpu.VMEM(inputs[1].shape, jnp.int32),
            pltpu.VMEM(inputs[2].shape, jnp.bfloat16),
            pltpu.SemaphoreType.DMA((2,)),
        ],
        compiler_params=grant(52 * 2**20) if resident else None,
        name="framed_weights",
        **extra,
    )(*inputs)


def pack(packed, slot, blocks, frames):
    rows, lanes = blocks[0].shape
    pairs = rows // frames
    for k, ref in enumerate(blocks):
        at = (slot * len(blocks) + k) * pairs
        for j in range(lanes // LANES):
            for f in range(frames):
                packed[j, pl.ds(at, pairs), pl.ds(f * LANES, LANES)] = ref[
                    pl.ds(f * pairs, pairs), pl.ds(j * LANES, LANES)
                ]


def settle(products, spread, merge):
    inputs = spread.shape[1] // 2
    v = bf_pair(jnp.concatenate(products, 0))
    u = sum(jnp.dot(x, spread, preferred_element_type=jnp.float32) for x in v)
    u = bf_pair(jnp.concatenate([u[:, :inputs], u[:, inputs:]], 0))
    return sum(jnp.dot(merge, x, preferred_element_type=jnp.float32) for x in u)


def near_kernel(owners, sections, frames, *refs):
    mine, twin = refs[:owners], refs[owners : 2 * owners]
    part_ref, packed, merge_ref, far_ref, theirs = refs[2 * owners :]
    width = packed.shape[0]
    pairs = mine[0].shape[0] // frames
    block = owners * pairs
    members = block // 2
    inputs = part_ref.shape[1]
    here, section, pol = lax.axis_index("chan"), lax.axis_index("stat"), lax.axis_index("pol")
    pack(packed, 0, mine, frames)
    pack(theirs, 0, twin, frames)
    one, zero = jnp.float32(1), jnp.float32(0)

    def spread_of(slots, source, there):
        col = lax.broadcasted_iota(jnp.int32, (slots * block, 1), 0)
        slot, inner = split_low(col, block)
        k, rest = split_low(inner, pairs)
        target = (source(slot) * 2 + there(slot)) * members + (here ^ k) * (pairs // 2) + (rest >> 1)
        wide = lax.broadcasted_iota(jnp.int32, (slots * block, 2 * inputs), 1)
        return jnp.where(wide == target + (rest & 1) * inputs, one, zero).astype(jnp.bfloat16)

    near = spread_of(2, lambda slot: section, lambda slot: pol ^ slot)
    far_ref[...] = spread_of(
        2 * (sections - 1), lambda slot: section ^ ((slot >> 1) + 1), lambda slot: pol ^ (slot & 1)
    )
    height = width * block
    left = lax.broadcasted_iota(jnp.int32, (height, height), 0)
    right = lax.broadcasted_iota(jnp.int32, (1, height), 1)
    j, inner = split_low(right, block)
    k, rest = split_low(inner, pairs)
    aim = j * block + (here ^ k) * (pairs // 2) + (rest >> 1)
    part = rest & 1
    scale = jnp.float32(1)
    merge_ref[:, :height] = jnp.where(left == aim + part * members, scale, zero).astype(jnp.bfloat16)
    sign = jnp.where(part == 1, scale, -scale)
    merge_ref[:, height:] = jnp.where(left == aim + (1 - part) * members, sign, zero).astype(jnp.bfloat16)
    products = [
        jnp.concatenate([dot_tt(packed[j], packed[j]), dot_tt(packed[j], theirs[j])], 1) for j in range(width)
    ]
    part_ref[...] = settle(products, near, merge_ref[...]) * (1.0 / (frames * LANES))


def correlate_near(mine, twin, frames, sections):
    owners = len(mine)
    rows, lanes = mine[0].shape
    width, block = lanes // LANES, owners * rows // frames
    inputs = block * sections
    bf = jnp.bfloat16
    return pl.pallas_call(
        functools.partial(near_kernel, owners, sections, frames),
        out_shape=[
            jax.ShapeDtypeStruct((width * block, inputs), jnp.float32),
            jax.ShapeDtypeStruct((width, block, frames * LANES), bf),
            jax.ShapeDtypeStruct((width * block, 2 * width * block), bf),
            jax.ShapeDtypeStruct((2 * (sections - 1) * block, 2 * inputs), bf),
        ],
        in_specs=whole_vmem(2 * owners),
        out_specs=whole_vmem(4),
        scratch_shapes=[pltpu.VMEM((width, block, frames * LANES), bf)],
        compiler_params=grant(),
        name="correlate_near",
    )(*mine, *twin)


def far_products(packed, theirs, others, frames):
    for slot, blocks in enumerate(others):
        pack(theirs, slot, blocks, frames)
    return [dot_tt(packed[j], theirs[j]) for j in range(packed.shape[0])]


def gather_rows(data, blocks, owners, sections):
    rows = blocks[0].shape[0]
    here, section = lax.axis_index("chan"), lax.axis_index("stat")
    for x in range(sections):
        for k in range(owners):
            at = ((section ^ x) * owners + (here ^ k)) * rows
            data[pl.ds(pl.multiple_of(at, rows), rows), :] = blocks[x * owners + k][...]


def finish_kernel(owners, sections, frames, share, span, weight_ref, part_ref, packed, merge_ref, far_ref, *refs):
    count = owners * sections
    blocks, crossed = refs[:count], refs[count : 2 * count - owners]
    out_ref, vis_ref, data, theirs, vis, held, sems, *chunk = refs[2 * count - owners :]
    slots = held.shape[0]
    height, lanes = out_ref.shape
    steps = [(row, lane) for row in range(0, height, share) for lane in range(0, lanes, span)]
    vis_copy = pltpu.make_async_copy(vis, vis_ref, sems.at[slots])

    def copy(i):
        row, lane = steps[i]
        return pltpu.make_async_copy(
            held.at[i % slots], out_ref.at[pl.ds(row, share), pl.ds(lane, span)], sems.at[i % slots]
        )

    gather_rows(data, blocks, owners, sections)
    for i, (row, lane) in enumerate(steps):
        if i >= slots:
            copy(i - slots).wait()
        if chunk:
            load = pltpu.make_async_copy(weight_ref.at[pl.ds(row, share)], chunk[0], sems.at[slots + 1])
            load.start()
            load.wait()
            weights = chunk[0][...]
        else:
            weights = weight_ref[row : row + share, :]
        held[i % slots] = jnp.dot(weights, data[:, lane : lane + span], preferred_element_type=jnp.float32)
        copy(i).start()
        if i == min(slots, len(steps)) - 1:
            others = []
            for x in range(1, sections):
                others.append(blocks[x * owners : (x + 1) * owners])
                others.append(crossed[(x - 1) * owners : x * owners])
            products = far_products(packed, theirs, others, frames)
            vis[...] = part_ref[...] + settle(products, far_ref[...], merge_ref[...]) * (1.0 / (frames * LANES))
            vis_copy.start()
    for i in range(max(0, len(steps) - slots), len(steps)):
        copy(i).wait()
    vis_copy.wait()


def finish(weights, near, mine, others, crossed, frames, sections):
    owners = len(mine)
    height, depth = weights.shape
    _, lanes = mine[0].shape
    part, packed, merge, far = near
    width, block, length = packed.shape
    resident = height * depth * 2 <= RESIDENT
    span = min(lanes, 512)
    share = 8 * pieces(height // 8, 100 if resident else 25)
    slots = 4
    weight_spec = pl.BlockSpec(memory_space=pltpu.VMEM if resident else pltpu.HBM)
    chunk = [] if resident else [pltpu.VMEM((share, depth), jnp.bfloat16)]
    return pl.pallas_call(
        functools.partial(finish_kernel, owners, sections, frames, share, span),
        out_shape=[jax.ShapeDtypeStruct((height, lanes), jnp.float32), jax.ShapeDtypeStruct(part.shape, jnp.float32)],
        in_specs=[weight_spec] + whole_vmem(4 + 2 * len(others) + owners),
        out_specs=[pl.BlockSpec(memory_space=pl.ANY)] * 2,
        scratch_shapes=[
            pltpu.VMEM((depth, lanes), jnp.bfloat16),
            pltpu.VMEM((width, 2 * (sections - 1) * block, length), jnp.bfloat16),
            pltpu.VMEM(part.shape, jnp.float32),
            pltpu.VMEM((slots, share, span), jnp.float32),
            pltpu.SemaphoreType.DMA((slots + 2,)),
        ]
        + chunk,
        compiler_params=grant() if resident else None,
        name="finish",
    )(weights, part, packed, merge, far, *mine, *others, *crossed)


def partner(x, axis, distance):
    return lax.ppermute(x, axis, [(i, i ^ distance) for i in range(lax.axis_size(axis))])


def moved(parts, axis, distance):
    if len(parts) == 1:
        return [partner(parts[0], axis, distance)]
    return jnp.split(partner(jnp.concatenate(parts, 0), axis, distance), len(parts), 0)


def on_device(voltages, filter_taps, beam_table, beam_index, block_owner):
    owners, sections = lax.axis_size("chan"), lax.axis_size("stat")
    stations = voltages.shape[1]
    frames = voltages.shape[3] - filter_taps.shape[0] + 1
    pairs = 2 * stations
    groups = block_owner.shape[0]
    owned = beam_index.shape[0] // sections
    own = channelise(voltages, filter_taps, block_owner, owners)
    weights = framed_weights(beam_table, beam_index, frames, pairs, owned)
    mine = [own[0]] + [partner(own[k], "chan", k) for k in range(1, owners)]
    lead = max(1, owners // 4)
    twin, others, crossed = [], [[] for _ in range(1, sections)], [[] for _ in range(1, sections)]
    for g in range(owners // lead):
        part = mine[g * lead : (g + 1) * lead]
        twin += moved(part, "pol", 1)
        for x in range(1, sections):
            far = moved(part, "stat", x)
            others[x - 1] += far
            crossed[x - 1] += moved(far, "pol", 1)
    near = correlate_near(mine, twin, frames, sections)
    beams, vis = finish(weights, near, mine, sum(others, []), sum(crossed, []), frames, sections)
    vis = vis.reshape(groups // owners, 2, -1, vis.shape[1])
    return vis, beams.reshape(owned, 1, 2, frames, -1)


def solution(mesh):
    return jax.shard_map(
        on_device,
        mesh=mesh,
        in_specs=(P(("group", "stat"), "chan", "pol", None, None, None), P(), P(), P(), P()),
        out_specs=(
            P(("group", "chan"), None, ("stat", "pol"), None),
            P(("group", "stat"), "pol", None, None, "chan"),
        ),
        check_vma=False,
    )
```

```python
import functools, math
import jax, jax.numpy as jnp, numpy as np
from jax import lax
from jax.experimental import pallas as pl
from jax.experimental.pallas import tpu as pltpu
from jax.sharding import PartitionSpec as P


LANES = 128
HALF = 4


def dft_parts(rows, cols, length):
    phase = np.outer(np.arange(rows), np.arange(cols)) % length * (2.0 * np.pi / length)
    return np.cos(phase), np.sin(phase)


def channel_tables(nfft, groups):
    depth = nfft // LANES
    per_group = LANES // depth
    cosine, sine = dft_parts(depth, depth, depth)
    pair = np.stack([np.stack([cosine, sine], -1), np.stack([-sine, cosine], -1)])
    first = np.einsum("akrc,fg->afkgrc", pair, np.eye(HALF))
    first = first.reshape(2 * HALF * depth, HALF * depth * 2)
    turn_cos, turn_sin = dft_parts(depth, LANES, nfft)
    cosine, sine = dft_parts(LANES, LANES, LANES)
    order = (np.arange(groups)[None, :] * per_group + np.arange(per_group)[:, None]).reshape(-1)
    cosine, sine = cosine[order] / math.sqrt(nfft), sine[order] / math.sqrt(nfft)
    second = np.concatenate([np.concatenate([cosine, sine], 1), np.concatenate([-sine, cosine], 1)], 0)
    spread = np.einsum("qr,fg,kl->qfkgrl", np.eye(per_group), np.eye(HALF), np.eye(depth))
    spread = spread.reshape(per_group * HALF * depth, HALF * per_group * depth)
    bf = lambda x: jnp.asarray(x, jnp.bfloat16)
    return bf(first), jnp.asarray(np.stack([turn_cos, turn_sin]), jnp.float32), bf(second), bf(spread)


def channel_kernel(owners, owner_hbm, volt_ref, taps_hbm, first_ref, turn_ref, second_ref, spread_ref, *rest):
    outs = rest[:owners]
    owner_ref, volts, taps_ref, tap_rows, first, turn, second, spread, filt, wide, pick, sems = rest[owners:]
    stations, blocks, rows, _ = volt_ref.shape
    taps = taps_ref.shape[0]
    frames = blocks - taps + 1
    halves = frames // HALF
    depth = rows // 2
    groups = owner_hbm.shape[0]
    width = groups // owners
    quads = LANES // depth
    span = HALF * depth
    here = lax.axis_index("chan")
    tap_copy = pltpu.make_async_copy(taps_hbm, taps_ref, sems.at[stations + 4])
    tap_copy.start()
    owner_copy = pltpu.make_async_copy(owner_hbm, owner_ref, sems.at[stations + 5])
    owner_copy.start()
    copies = []
    for s in range(stations):
        copies.append(pltpu.make_async_copy(volt_ref.at[s], volts.at[s], sems.at[s]))
    consts = []
    for i, (src, dst) in enumerate([(first_ref, first), (turn_ref, turn), (second_ref, second), (spread_ref, spread)]):
        consts.append(pltpu.make_async_copy(src, dst, sems.at[stations + i]))
    for c in copies + consts:
        c.start()
    tap_copy.wait()

    sub = lax.broadcasted_iota(jnp.int32, (8, LANES), 0)
    for t in range(taps):
        for m in range(rows // 8):
            parts = [jnp.broadcast_to(taps_ref[t : t + 1, pl.ds((4 * m + i) * LANES, LANES)], (8, LANES)) for i in range(4)]
            low = jnp.where(sub < 2, parts[0], parts[1])
            high = jnp.where(sub < 6, parts[2], parts[3])
            tap_rows[t, pl.ds(8 * m, 8), :] = jnp.where(sub < 4, low, high)

    owner_copy.wait()
    sc = 2 * stations
    lane = lax.broadcasted_iota(jnp.int32, (sc, sc * groups), 1)
    base = lax.broadcasted_iota(jnp.int32, (sc, sc * groups), 0) * groups
    for k in range(owners):
        for j in range(width):
            g = owner_ref[(here ^ k) * width + j]
            p = (k * width + j) * sc
            pick[pl.ds(p, sc), :] = jnp.where(lane == base + g, 1.0, 0.0).astype(jnp.bfloat16)

    step = 16
    for s in range(stations):
        copies[s].wait()

        def fir(m, carry, s=s):
            at = pl.multiple_of(m * step, step)
            x = [volts[s, b, pl.ds(at, step), :].astype(jnp.float32) for b in range(blocks)]
            w = [tap_rows[t, pl.ds(at, step), :] for t in range(taps)]
            for f in range(frames):
                total = w[0] * x[f]
                for t in range(1, taps):
                    total = total + w[t] * x[f + t]
                row = pl.multiple_of((f % HALF) * rows + at, step)
                filt[s, pl.ds(row, step), pl.ds((f // HALF) * LANES, LANES)] = total.astype(jnp.bfloat16)
            return carry

        lax.fori_loop(0, rows // step, fir, 0)

    for c in consts:
        c.wait()
    f32 = jnp.float32
    cosine = jnp.concatenate([turn[0]] * HALF, 0)
    sine = jnp.concatenate([turn[1]] * HALF, 0)
    for s in range(stations):
        y = jnp.dot(first[...], filt[s], preferred_element_type=f32)
        re, im = y[:span], y[span:]
        turned = []
        for h in range(halves):
            a, b = re[:, h * LANES : (h + 1) * LANES], im[:, h * LANES : (h + 1) * LANES]
            turned.append(jnp.concatenate([a * cosine + b * sine, b * cosine - a * sine], 1))
        turned = jnp.concatenate(turned, 0).astype(jnp.bfloat16)
        z = lax.dot_general(second[...], turned, (((1,), (1,)), ((), ())), preferred_element_type=f32).astype(jnp.bfloat16)
        for c in range(2):
            for q in range(quads):
                for h in range(halves):
                    wide[h, pl.ds((s * 2 + c) * groups, groups), pl.ds(q * LANES, LANES)] = z[
                        c * quads * groups + q * groups : c * quads * groups + (q + 1) * groups, h * LANES : (h + 1) * LANES
                    ]
    for h in range(halves):
        y = jnp.dot(wide[h], spread[...], preferred_element_type=f32).astype(jnp.bfloat16)
        z = jnp.dot(pick[...], y, preferred_element_type=f32)
        for k in range(owners):
            for j in range(width):
                for f in range(HALF):
                    p = (k * width + j) * sc
                    outs[k][pl.ds((h * HALF + f) * sc, sc), pl.ds(j * LANES, LANES)] = z[
                        p : p + sc, f * LANES : (f + 1) * LANES
                    ].astype(jnp.bfloat16)


def channelise(voltages, filter_taps, block_owner, owners):
    _, stations, _, blocks, _, nfft = voltages.shape
    taps = filter_taps.shape[0]
    frames = blocks - taps + 1
    groups = block_owner.shape[0]
    depth = nfft // LANES
    volts = voltages.reshape(stations, blocks, 2, depth, LANES).transpose(0, 1, 3, 2, 4).reshape(stations, blocks, 2 * depth, LANES)
    first, turn, second, spread = channel_tables(nfft, groups)
    sc = 2 * stations
    width = groups // owners
    inputs = (block_owner, volts, filter_taps, first, turn, second, spread)
    anyspec = pl.BlockSpec(memory_space=pltpu.HBM)
    bf = jnp.bfloat16
    return pl.pallas_call(
        functools.partial(channel_kernel, owners),
        out_shape=[jax.ShapeDtypeStruct((frames * sc, width * LANES), bf)] * owners,
        in_specs=[anyspec] * 7,
        out_specs=[pl.BlockSpec(memory_space=pltpu.VMEM)] * owners,
        scratch_shapes=[
            pltpu.SMEM(block_owner.shape, jnp.int32),
            pltpu.VMEM(volts.shape, bf),
            pltpu.VMEM(filter_taps.shape, jnp.float32),
            pltpu.VMEM((taps, 2 * depth, LANES), jnp.float32),
            pltpu.VMEM(first.shape, bf),
            pltpu.VMEM(turn.shape, jnp.float32),
            pltpu.VMEM(second.shape, bf),
            pltpu.VMEM(spread.shape, bf),
            pltpu.VMEM((stations, HALF * 2 * depth, frames // HALF * LANES), bf),
            pltpu.VMEM((frames // HALF, sc * groups, spread.shape[0]), bf),
            pltpu.VMEM((groups * sc, sc * groups), bf),
            pltpu.SemaphoreType.DMA((stations + 6,)),
        ],
        compiler_params=grant(),
        name="channelise",
    )(*[pltpu.with_memory_space_constraint(x, pltpu.HBM) for x in inputs])


VMEM_BYTES = 24 * 2**20
RESIDENT = 8 * 2**20
SLICE = 32


def whole_vmem(count):
    return [pl.BlockSpec(memory_space=pltpu.VMEM)] * count


def grant(size=VMEM_BYTES):
    return pltpu.CompilerParams(vmem_limit_bytes=size)


def pieces(total, most):
    return max(d for d in range(1, most + 1) if total % d == 0)


def split_low(x, size):
    shift = size.bit_length() - 1
    assert size == 1 << shift
    return x >> shift, x & (size - 1)


def bf_pair(x):
    high = x.astype(jnp.bfloat16)
    return high, (x - high.astype(jnp.float32)).astype(jnp.bfloat16)


def dot_tt(a, b):
    return lax.dot_general(a, b, (((1,), (1,)), ((), ())), preferred_element_type=jnp.float32)


def weights_kernel(pairs, owned, share, table_hbm, index_hbm, copy_hbm, out_ref, rows_ref, table_ref, index_ref, copy_ref, sems):
    stations, beams = index_ref.shape
    tile, spread = copy_ref.shape
    frames = spread // tile
    count = 2 * owned
    start = lax.axis_index("stat") * owned
    factor = 1.0 / math.sqrt(stations)

    def prepare():
        pairs_of = zip((table_hbm, index_hbm, copy_hbm), (table_ref, index_ref, copy_ref))
        loads = [pltpu.make_async_copy(src, dst, sems.at[i]) for i, (src, dst) in enumerate(pairs_of)]
        for load in loads:
            load.start()
        for load in loads:
            load.wait()
        row = lax.broadcasted_iota(jnp.int32, (count, beams), 0)
        lane = lax.broadcasted_iota(jnp.int32, (count, beams), 1)
        hit = lane == start + (row >> 1)
        one, zero = jnp.float32(1), jnp.float32(0)
        choose = [jnp.where(hit & ((row & 1) == c), one, zero).astype(jnp.bfloat16) for c in range(2)]
        for i in range(stations // SLICE):
            index = index_ref[i * SLICE : (i + 1) * SLICE, :]
            real = jnp.zeros(index.shape, jnp.float32)
            imag = jnp.zeros(index.shape, jnp.float32)
            for e in range(table_ref.shape[1]):
                here = index == e
                real = jnp.where(here, jnp.broadcast_to(table_ref[0:1, e : e + 1], index.shape), real)
                imag = jnp.where(here, jnp.broadcast_to(table_ref[1:2, e : e + 1], index.shape), imag)
            real, imag = real * factor, imag * factor
            upper = jnp.concatenate([real, -imag], 0).astype(jnp.bfloat16)
            lower = jnp.concatenate([imag, real], 0).astype(jnp.bfloat16)
            w = dot_tt(choose[0], upper) + dot_tt(choose[1], lower)
            rows_ref[:, i * spread : (i + 1) * spread] = jnp.dot(
                w.astype(jnp.bfloat16), copy_ref[...], preferred_element_type=jnp.float32
            )

    first = 0
    if share == count:
        prepare()
    else:
        pl.when(pl.program_id(0) == 0)(prepare)
        first = pl.program_id(0) * share
    width = out_ref.shape[1]
    lane = lax.broadcasted_iota(jnp.int32, (frames, width), 1)
    mine = split_low(split_low(lane, pairs)[0], frames)[1] == lax.broadcasted_iota(jnp.int32, (frames, width), 0)

    def fill(i, carry):
        row = rows_ref[pl.ds(first + i, 1), :]
        out_ref[pl.ds(pl.multiple_of(i * frames, frames), frames), :] = jnp.where(
            mine, jnp.broadcast_to(row, (frames, width)), 0.0
        ).astype(jnp.bfloat16)
        return carry

    lax.fori_loop(0, share, fill, 0, unroll=pieces(share, 10))


def weight_inputs(beam_table, beam_index, frames, pairs):
    eye = np.eye
    copies = np.einsum("bp,sq,ct,f->cbspqft", eye(2 * SLICE // pairs), eye(pairs // 2), eye(2), np.ones(frames))
    copies = np.moveaxis(copies, (3, 5, 4, 6), (3, 4, 5, 6)).reshape(2 * SLICE, 2 * SLICE * frames)
    return beam_table, beam_index.T, jnp.asarray(copies, jnp.bfloat16)


def framed_weights(inputs, frames, pairs, owned):
    stations = inputs[1].shape[0]
    depth = 2 * stations * frames
    count = 2 * owned
    resident = count * frames * depth * 2 <= RESIDENT
    share = count if resident else pieces(count, 10)
    extra = {}
    if not resident:
        extra = dict(grid=(count // share,), out_specs=pl.BlockSpec((share * frames, depth), lambda i: (i, 0)))
    return pl.pallas_call(
        functools.partial(weights_kernel, pairs, owned, share),
        out_shape=jax.ShapeDtypeStruct((count * frames, depth), jnp.bfloat16),
        in_specs=[pl.BlockSpec(memory_space=pltpu.HBM)] * 3,
        scratch_shapes=[pltpu.VMEM((count, depth), jnp.float32)]
        + [pltpu.VMEM(x.shape, x.dtype) for x in inputs]
        + [pltpu.SemaphoreType.DMA((3,))],
        compiler_params=grant() if resident else None,
        name="framed_weights",
        **extra,
    )(*[pltpu.with_memory_space_constraint(x, pltpu.HBM) for x in inputs])


def pack(packed, slot, blocks, frames):
    rows, lanes = blocks[0].shape
    pairs = rows // frames
    for k, ref in enumerate(blocks):
        at = (slot * len(blocks) + k) * pairs
        for j in range(lanes // LANES):
            for f in range(frames):
                packed[j, pl.ds(at, pairs), pl.ds(f * LANES, LANES)] = ref[
                    pl.ds(f * pairs, pairs), pl.ds(j * LANES, LANES)
                ]


def settle(products, spread, merge):
    inputs = spread.shape[1] // 2
    v = bf_pair(jnp.concatenate(products, 0))
    u = sum(jnp.dot(x, spread, preferred_element_type=jnp.float32) for x in v)
    u = bf_pair(jnp.concatenate([u[:, :inputs], u[:, inputs:]], 0))
    return sum(jnp.dot(merge, x, preferred_element_type=jnp.float32) for x in u)


def near_kernel(owners, sections, frames, *refs):
    mine, twin = refs[:owners], refs[owners : 2 * owners]
    part_ref, packed, merge_ref, far_ref, theirs = refs[2 * owners :]
    width = packed.shape[0]
    pairs = mine[0].shape[0] // frames
    block = owners * pairs
    members = block // 2
    inputs = part_ref.shape[1]
    here, section, pol = lax.axis_index("chan"), lax.axis_index("stat"), lax.axis_index("pol")
    pack(packed, 0, mine, frames)
    pack(theirs, 0, twin, frames)
    one, zero = jnp.float32(1), jnp.float32(0)

    def spread_of(slots, source, there):
        col = lax.broadcasted_iota(jnp.int32, (slots * block, 1), 0)
        slot, inner = split_low(col, block)
        k, rest = split_low(inner, pairs)
        target = (source(slot) * 2 + there(slot)) * members + (here ^ k) * (pairs // 2) + (rest >> 1)
        wide = lax.broadcasted_iota(jnp.int32, (slots * block, 2 * inputs), 1)
        return jnp.where(wide == target + (rest & 1) * inputs, one, zero).astype(jnp.bfloat16)

    near = spread_of(2, lambda slot: section, lambda slot: pol ^ slot)
    far_ref[...] = spread_of(
        2 * (sections - 1), lambda slot: section ^ ((slot >> 1) + 1), lambda slot: pol ^ (slot & 1)
    )
    height = width * block
    left = lax.broadcasted_iota(jnp.int32, (height, height), 0)
    right = lax.broadcasted_iota(jnp.int32, (1, height), 1)
    j, inner = split_low(right, block)
    k, rest = split_low(inner, pairs)
    aim = j * block + (here ^ k) * (pairs // 2) + (rest >> 1)
    part = rest & 1
    scale = jnp.float32(1)
    merge_ref[:, :height] = jnp.where(left == aim + part * members, scale, zero).astype(jnp.bfloat16)
    sign = jnp.where(part == 1, scale, -scale)
    merge_ref[:, height:] = jnp.where(left == aim + (1 - part) * members, sign, zero).astype(jnp.bfloat16)
    products = [
        jnp.concatenate([dot_tt(packed[j], packed[j]), dot_tt(packed[j], theirs[j])], 1) for j in range(width)
    ]
    part_ref[...] = settle(products, near, merge_ref[...]) * (1.0 / (frames * LANES))


def correlate_near(mine, twin, frames, sections):
    owners = len(mine)
    rows, lanes = mine[0].shape
    width, block = lanes // LANES, owners * rows // frames
    inputs = block * sections
    bf = jnp.bfloat16
    return pl.pallas_call(
        functools.partial(near_kernel, owners, sections, frames),
        out_shape=[
            jax.ShapeDtypeStruct((width * block, inputs), jnp.float32),
            jax.ShapeDtypeStruct((width, block, frames * LANES), bf),
            jax.ShapeDtypeStruct((width * block, 2 * width * block), bf),
            jax.ShapeDtypeStruct((2 * (sections - 1) * block, 2 * inputs), bf),
        ],
        in_specs=whole_vmem(2 * owners),
        out_specs=whole_vmem(4),
        scratch_shapes=[pltpu.VMEM((width, block, frames * LANES), bf)],
        compiler_params=grant(),
        name="correlate_near",
    )(*mine, *twin)


def far_products(packed, theirs, others, frames):
    for slot, blocks in enumerate(others):
        pack(theirs, slot, blocks, frames)
    return [dot_tt(packed[j], theirs[j]) for j in range(packed.shape[0])]


def gather_rows(data, blocks, owners, sections):
    rows = blocks[0].shape[0]
    here, section = lax.axis_index("chan"), lax.axis_index("stat")
    for x in range(sections):
        for k in range(owners):
            at = ((section ^ x) * owners + (here ^ k)) * rows
            data[pl.ds(pl.multiple_of(at, rows), rows), :] = blocks[x * owners + k][...]


def finish_kernel(owners, sections, frames, share, span, weight_ref, part_ref, packed, merge_ref, far_ref, *refs):
    count = owners * sections
    blocks, crossed = refs[:count], refs[count : 2 * count - owners]
    out_ref, vis_ref, data, theirs, vis, held, sems, *chunk = refs[2 * count - owners :]
    slots = held.shape[0]
    height, lanes = out_ref.shape
    steps = [(row, lane) for row in range(0, height, share) for lane in range(0, lanes, span)]
    vis_copy = pltpu.make_async_copy(vis, vis_ref, sems.at[slots])

    def copy(i):
        row, lane = steps[i]
        return pltpu.make_async_copy(
            held.at[i % slots], out_ref.at[pl.ds(row, share), pl.ds(lane, span)], sems.at[i % slots]
        )

    gather_rows(data, blocks, owners, sections)
    for i, (row, lane) in enumerate(steps):
        if i >= slots:
            copy(i - slots).wait()
        if chunk:
            load = pltpu.make_async_copy(weight_ref.at[pl.ds(row, share)], chunk[0], sems.at[slots + 1])
            load.start()
            load.wait()
            weights = chunk[0][...]
        else:
            weights = weight_ref[row : row + share, :]
        held[i % slots] = jnp.dot(weights, data[:, lane : lane + span], preferred_element_type=jnp.float32)
        copy(i).start()
        if i == min(slots, len(steps)) - 1:
            others = []
            for x in range(1, sections):
                others.append(blocks[x * owners : (x + 1) * owners])
                others.append(crossed[(x - 1) * owners : x * owners])
            products = far_products(packed, theirs, others, frames)
            vis[...] = part_ref[...] + settle(products, far_ref[...], merge_ref[...]) * (1.0 / (frames * LANES))
            vis_copy.start()
    for i in range(max(0, len(steps) - slots), len(steps)):
        copy(i).wait()
    vis_copy.wait()


def finish(weights, near, mine, others, crossed, frames, sections):
    owners = len(mine)
    height, depth = weights.shape
    _, lanes = mine[0].shape
    part, packed, merge, far = near
    width, block, length = packed.shape
    resident = height * depth * 2 <= RESIDENT
    span = min(lanes, 512)
    share = 8 * pieces(height // 8, 100 if resident else 25)
    slots = 4
    weight_spec = pl.BlockSpec(memory_space=pltpu.VMEM if resident else pltpu.HBM)
    chunk = [] if resident else [pltpu.VMEM((share, depth), jnp.bfloat16)]
    return pl.pallas_call(
        functools.partial(finish_kernel, owners, sections, frames, share, span),
        out_shape=[jax.ShapeDtypeStruct((height, lanes), jnp.float32), jax.ShapeDtypeStruct(part.shape, jnp.float32)],
        in_specs=[weight_spec] + whole_vmem(4 + 2 * len(others) + owners),
        out_specs=[pl.BlockSpec(memory_space=pl.ANY)] * 2,
        scratch_shapes=[
            pltpu.VMEM((depth, lanes), jnp.bfloat16),
            pltpu.VMEM((width, 2 * (sections - 1) * block, length), jnp.bfloat16),
            pltpu.VMEM(part.shape, jnp.float32),
            pltpu.VMEM((slots, share, span), jnp.float32),
            pltpu.SemaphoreType.DMA((slots + 2,)),
        ]
        + chunk,
        compiler_params=grant() if resident else None,
        name="finish",
    )(weights, part, packed, merge, far, *mine, *others, *crossed)


def partner(x, axis, distance):
    return lax.ppermute(x, axis, [(i, i ^ distance) for i in range(lax.axis_size(axis))])


def moved(parts, axis, distance):
    if len(parts) == 1:
        return [partner(parts[0], axis, distance)]
    return jnp.split(partner(jnp.concatenate(parts, 0), axis, distance), len(parts), 0)


def on_device(voltages, filter_taps, beam_table, beam_index, block_owner):
    owners, sections = lax.axis_size("chan"), lax.axis_size("stat")
    stations = voltages.shape[1]
    frames = voltages.shape[3] - filter_taps.shape[0] + 1
    pairs = 2 * stations
    groups = block_owner.shape[0]
    owned = beam_index.shape[0] // sections
    tables = weight_inputs(beam_table, beam_index, frames, pairs)
    own = channelise(voltages, filter_taps, block_owner, owners)
    weights = framed_weights(tables, frames, pairs, owned)
    mine = [own[0]] + [partner(own[k], "chan", k) for k in range(1, owners)]
    lead = max(1, owners // 4)
    twin, others, crossed = [], [[] for _ in range(1, sections)], [[] for _ in range(1, sections)]
    for g in range(owners // lead):
        part = mine[g * lead : (g + 1) * lead]
        twin += moved(part, "pol", 1)
        for x in range(1, sections):
            far = moved(part, "stat", x)
            others[x - 1] += far
            crossed[x - 1] += moved(far, "pol", 1)
    near = correlate_near(mine, twin, frames, sections)
    beams, vis = finish(weights, near, mine, sum(others, []), sum(crossed, []), frames, sections)
    vis = vis.reshape(groups // owners, 2, -1, vis.shape[1])
    return vis, beams.reshape(owned, 1, 2, frames, -1)


def solution(mesh):
    return jax.shard_map(
        on_device,
        mesh=mesh,
        in_specs=(P(("group", "stat"), "chan", "pol", None, None, None), P(), P(), P(), P()),
        out_specs=(
            P(("group", "chan"), None, ("stat", "pol"), None),
            P(("group", "stat"), "pol", None, None, "chan"),
        ),
        check_vma=False,
    )
```

```python
import functools, math
import jax, jax.numpy as jnp, numpy as np
from jax import lax
from jax.experimental import pallas as pl
from jax.experimental.pallas import tpu as pltpu
from jax.sharding import PartitionSpec as P


LANES = 128
HALF = 4


def dft_parts(rows, cols, length):
    phase = np.outer(np.arange(rows), np.arange(cols)) % length * (2.0 * np.pi / length)
    return np.cos(phase), np.sin(phase)


def channel_tables(nfft, groups):
    depth = nfft // LANES
    per_group = LANES // depth
    cosine, sine = dft_parts(depth, depth, depth)
    pair = np.stack([np.stack([cosine, sine], -1), np.stack([-sine, cosine], -1)])
    first = np.einsum("akrc,fg->afkgrc", pair, np.eye(HALF))
    first = first.reshape(2 * HALF * depth, HALF * depth * 2)
    turn_cos, turn_sin = dft_parts(depth, LANES, nfft)
    cosine, sine = dft_parts(LANES, LANES, LANES)
    order = (np.arange(groups)[None, :] * per_group + np.arange(per_group)[:, None]).reshape(-1)
    cosine, sine = cosine[order] / math.sqrt(nfft), sine[order] / math.sqrt(nfft)
    second = np.concatenate([np.concatenate([cosine, sine], 1), np.concatenate([-sine, cosine], 1)], 0)
    spread = np.einsum("qr,fg,kl->qfkgrl", np.eye(per_group), np.eye(HALF), np.eye(depth))
    spread = spread.reshape(per_group * HALF * depth, HALF * per_group * depth)
    bf = lambda x: jnp.asarray(x, jnp.bfloat16)
    return bf(first), jnp.asarray(np.stack([turn_cos, turn_sin]), jnp.float32), bf(second), bf(spread)


def channel_kernel(owners, paired, owner_hbm, volt_ref, taps_hbm, first_ref, turn_ref, second_ref, spread_ref, *rest):
    passed, outs, handed = rest[:3], rest[3 : 3 + owners + paired], rest[3 + owners + paired : 6 + owners + paired]
    owner_ref, volts, taps_ref, tap_rows, first, turn, second, spread, filt, wide, pick, sems = rest[6 + owners + paired :]
    stations, blocks, rows, _ = volt_ref.shape
    taps = taps_ref.shape[0]
    frames = blocks - taps + 1
    halves = frames // HALF
    depth = rows // 2
    groups = owner_hbm.shape[0]
    width = groups // owners
    quads = LANES // depth
    span = HALF * depth
    here = lax.axis_index("chan")
    tap_copy = pltpu.make_async_copy(taps_hbm, taps_ref, sems.at[stations + 4])
    tap_copy.start()
    owner_copy = pltpu.make_async_copy(owner_hbm, owner_ref, sems.at[stations + 5])
    owner_copy.start()
    copies = []
    for s in range(stations):
        copies.append(pltpu.make_async_copy(volt_ref.at[s], volts.at[s], sems.at[s]))
    consts = []
    for i, (src, dst) in enumerate([(first_ref, first), (turn_ref, turn), (second_ref, second), (spread_ref, spread)]):
        consts.append(pltpu.make_async_copy(src, dst, sems.at[stations + i]))
    for i, (src, dst) in enumerate(zip(passed, handed)):
        consts.append(pltpu.make_async_copy(src, dst, sems.at[stations + 6 + i]))
    for c in copies + consts:
        c.start()
    tap_copy.wait()

    sub = lax.broadcasted_iota(jnp.int32, (8, LANES), 0)
    for t in range(taps):
        for m in range(rows // 8):
            parts = [jnp.broadcast_to(taps_ref[t : t + 1, pl.ds((4 * m + i) * LANES, LANES)], (8, LANES)) for i in range(4)]
            low = jnp.where(sub < 2, parts[0], parts[1])
            high = jnp.where(sub < 6, parts[2], parts[3])
            tap_rows[t, pl.ds(8 * m, 8), :] = jnp.where(sub < 4, low, high)

    owner_copy.wait()
    sc = 2 * stations
    lane = lax.broadcasted_iota(jnp.int32, (sc, sc * groups), 1)
    base = lax.broadcasted_iota(jnp.int32, (sc, sc * groups), 0) * groups
    for k in range(owners):
        for j in range(width):
            g = owner_ref[(here ^ k) * width + j]
            p = (k * width + j) * sc
            pick[pl.ds(p, sc), :] = jnp.where(lane == base + g, 1.0, 0.0).astype(jnp.bfloat16)

    step = 16
    for s in range(stations):
        copies[s].wait()

        def fir(m, carry, s=s):
            at = pl.multiple_of(m * step, step)
            x = [volts[s, b, pl.ds(at, step), :].astype(jnp.float32) for b in range(blocks)]
            w = [tap_rows[t, pl.ds(at, step), :] for t in range(taps)]
            for f in range(frames):
                total = w[0] * x[f]
                for t in range(1, taps):
                    total = total + w[t] * x[f + t]
                row = pl.multiple_of((f % HALF) * rows + at, step)
                filt[s, pl.ds(row, step), pl.ds((f // HALF) * LANES, LANES)] = total.astype(jnp.bfloat16)
            return carry

        lax.fori_loop(0, rows // step, fir, 0)

    for c in consts:
        c.wait()
    f32 = jnp.float32
    cosine = jnp.concatenate([turn[0]] * HALF, 0)
    sine = jnp.concatenate([turn[1]] * HALF, 0)
    for s in range(stations):
        y = jnp.dot(first[...], filt[s], preferred_element_type=f32)
        re, im = y[:span], y[span:]
        turned = []
        for h in range(halves):
            a, b = re[:, h * LANES : (h + 1) * LANES], im[:, h * LANES : (h + 1) * LANES]
            turned.append(jnp.concatenate([a * cosine + b * sine, b * cosine - a * sine], 1))
        turned = jnp.concatenate(turned, 0).astype(jnp.bfloat16)
        z = lax.dot_general(second[...], turned, (((1,), (1,)), ((), ())), preferred_element_type=f32).astype(jnp.bfloat16)
        for c in range(2):
            for q in range(quads):
                for h in range(halves):
                    wide[h, pl.ds((s * 2 + c) * groups, groups), pl.ds(q * LANES, LANES)] = z[
                        c * quads * groups + q * groups : c * quads * groups + (q + 1) * groups, h * LANES : (h + 1) * LANES
                    ]
    for h in range(halves):
        y = jnp.dot(wide[h], spread[...], preferred_element_type=f32).astype(jnp.bfloat16)
        z = jnp.dot(pick[...], y, preferred_element_type=f32)
        for k in range(owners):
            for j in range(width):
                for f in range(HALF):
                    p = (k * width + j) * sc
                    block = z[p : p + sc, f * LANES : (f + 1) * LANES].astype(jnp.bfloat16)
                    row = (h * HALF + f) * sc
                    outs[k][pl.ds(row, sc), pl.ds(j * LANES, LANES)] = block
                    if paired and k < 2:
                        outs[owners][pl.ds(k * frames * sc + row, sc), pl.ds(j * LANES, LANES)] = block


def channelise(voltages, filter_taps, block_owner, owners, paired, passed):
    _, stations, _, blocks, _, nfft = voltages.shape
    taps = filter_taps.shape[0]
    frames = blocks - taps + 1
    groups = block_owner.shape[0]
    depth = nfft // LANES
    volts = voltages.reshape(stations, blocks, 2, depth, LANES).transpose(0, 1, 3, 2, 4).reshape(stations, blocks, 2 * depth, LANES)
    first, turn, second, spread = channel_tables(nfft, groups)
    sc = 2 * stations
    width = groups // owners
    inputs = (block_owner, volts, filter_taps, first, turn, second, spread, *passed)
    block = jax.ShapeDtypeStruct((frames * sc, width * LANES), jnp.bfloat16)
    pair = jax.ShapeDtypeStruct((2 * frames * sc, width * LANES), jnp.bfloat16)
    anyspec = pl.BlockSpec(memory_space=pltpu.HBM)
    bf = jnp.bfloat16
    return pl.pallas_call(
        functools.partial(channel_kernel, owners, paired),
        out_shape=[block] * owners + [pair] * paired + [jax.ShapeDtypeStruct(x.shape, x.dtype) for x in passed],
        in_specs=[anyspec] * len(inputs),
        out_specs=[pl.BlockSpec(memory_space=pltpu.VMEM)] * (owners + paired + len(passed)),
        scratch_shapes=[
            pltpu.SMEM(block_owner.shape, jnp.int32),
            pltpu.VMEM(volts.shape, bf),
            pltpu.VMEM(filter_taps.shape, jnp.float32),
            pltpu.VMEM((taps, 2 * depth, LANES), jnp.float32),
            pltpu.VMEM(first.shape, bf),
            pltpu.VMEM(turn.shape, jnp.float32),
            pltpu.VMEM(second.shape, bf),
            pltpu.VMEM(spread.shape, bf),
            pltpu.VMEM((stations, HALF * 2 * depth, frames // HALF * LANES), bf),
            pltpu.VMEM((frames // HALF, sc * groups, spread.shape[0]), bf),
            pltpu.VMEM((groups * sc, sc * groups), bf),
            pltpu.SemaphoreType.DMA((stations + 9,)),
        ],
        compiler_params=grant(),
        name="channelise",
    )(*[pltpu.with_memory_space_constraint(x, pltpu.HBM) for x in inputs])


VMEM_BYTES = 24 * 2**20
RESIDENT = 8 * 2**20
SLICE = 32


def whole_vmem(count):
    return [pl.BlockSpec(memory_space=pltpu.VMEM)] * count


def grant(size=VMEM_BYTES):
    return pltpu.CompilerParams(vmem_limit_bytes=size)


def pieces(total, most):
    return max(d for d in range(1, most + 1) if total % d == 0)


def split_low(x, size):
    shift = size.bit_length() - 1
    assert size == 1 << shift
    return x >> shift, x & (size - 1)


def bf_pair(x):
    high = x.astype(jnp.bfloat16)
    return high, (x - high.astype(jnp.float32)).astype(jnp.bfloat16)


def dot_tt(a, b):
    return lax.dot_general(a, b, (((1,), (1,)), ((), ())), preferred_element_type=jnp.float32)


def weights_kernel(pairs, owned, share, table_ref, index_ref, copy_ref, out_ref, rows_ref):
    stations, beams = index_ref.shape
    tile, spread = copy_ref.shape
    frames = spread // tile
    count = 2 * owned
    start = lax.axis_index("stat") * owned
    factor = 1.0 / math.sqrt(stations)

    def prepare():
        row = lax.broadcasted_iota(jnp.int32, (count, beams), 0)
        lane = lax.broadcasted_iota(jnp.int32, (count, beams), 1)
        hit = lane == start + (row >> 1)
        one, zero = jnp.float32(1), jnp.float32(0)
        choose = [jnp.where(hit & ((row & 1) == c), one, zero).astype(jnp.bfloat16) for c in range(2)]
        for i in range(stations // SLICE):
            index = index_ref[i * SLICE : (i + 1) * SLICE, :]
            real = jnp.zeros(index.shape, jnp.float32)
            imag = jnp.zeros(index.shape, jnp.float32)
            for e in range(table_ref.shape[1]):
                here = index == e
                real = jnp.where(here, jnp.broadcast_to(table_ref[0:1, e : e + 1], index.shape), real)
                imag = jnp.where(here, jnp.broadcast_to(table_ref[1:2, e : e + 1], index.shape), imag)
            real, imag = real * factor, imag * factor
            upper = jnp.concatenate([real, -imag], 0).astype(jnp.bfloat16)
            lower = jnp.concatenate([imag, real], 0).astype(jnp.bfloat16)
            w = dot_tt(choose[0], upper) + dot_tt(choose[1], lower)
            rows_ref[:, i * spread : (i + 1) * spread] = jnp.dot(
                w.astype(jnp.bfloat16), copy_ref[...], preferred_element_type=jnp.float32
            )

    first = 0
    if share == count:
        prepare()
    else:
        pl.when(pl.program_id(0) == 0)(prepare)
        first = pl.program_id(0) * share
    width = out_ref.shape[1]
    lane = lax.broadcasted_iota(jnp.int32, (frames, width), 1)
    mine = split_low(split_low(lane, pairs)[0], frames)[1] == lax.broadcasted_iota(jnp.int32, (frames, width), 0)

    def fill(i, carry):
        row = rows_ref[pl.ds(first + i, 1), :]
        out_ref[pl.ds(pl.multiple_of(i * frames, frames), frames), :] = jnp.where(
            mine, jnp.broadcast_to(row, (frames, width)), 0.0
        ).astype(jnp.bfloat16)
        return carry

    lax.fori_loop(0, share, fill, 0, unroll=pieces(share, 10))


def weight_inputs(beam_table, beam_index, frames, pairs):
    eye = np.eye
    copies = np.einsum("bp,sq,ct,f->cbspqft", eye(2 * SLICE // pairs), eye(pairs // 2), eye(2), np.ones(frames))
    copies = np.moveaxis(copies, (3, 5, 4, 6), (3, 4, 5, 6)).reshape(2 * SLICE, 2 * SLICE * frames)
    return beam_table, beam_index.T, jnp.asarray(copies, jnp.bfloat16)


def framed_weights(inputs, frames, pairs, owned):
    stations = inputs[1].shape[0]
    depth = 2 * stations * frames
    count = 2 * owned
    resident = count * frames * depth * 2 <= RESIDENT
    share = count if resident else pieces(count, 10)
    extra = {}
    if not resident:
        extra = dict(grid=(count // share,), out_specs=pl.BlockSpec((share * frames, depth), lambda i: (i, 0)))
    return pl.pallas_call(
        functools.partial(weights_kernel, pairs, owned, share),
        out_shape=jax.ShapeDtypeStruct((count * frames, depth), jnp.bfloat16),
        in_specs=whole_vmem(3),
        scratch_shapes=[pltpu.VMEM((count, depth), jnp.float32)],
        compiler_params=grant() if resident else None,
        name="framed_weights",
        **extra,
    )(*inputs)


def pack(packed, slot, blocks, frames):
    rows, lanes = blocks[0].shape
    pairs = rows // frames
    for k, ref in enumerate(blocks):
        at = (slot * len(blocks) + k) * pairs
        for j in range(lanes // LANES):
            for f in range(frames):
                packed[j, pl.ds(at, pairs), pl.ds(f * LANES, LANES)] = ref[
                    pl.ds(f * pairs, pairs), pl.ds(j * LANES, LANES)
                ]


def settle(products, spread, merge):
    inputs = spread.shape[1] // 2
    v = bf_pair(jnp.concatenate(products, 0))
    u = sum(jnp.dot(x, spread, preferred_element_type=jnp.float32) for x in v)
    u = bf_pair(jnp.concatenate([u[:, :inputs], u[:, inputs:]], 0))
    return sum(jnp.dot(merge, x, preferred_element_type=jnp.float32) for x in u)


def near_kernel(owners, sections, frames, *refs):
    mine, twin = refs[:owners], refs[owners : 2 * owners]
    part_ref, packed, merge_ref, far_ref, theirs = refs[2 * owners :]
    width = packed.shape[0]
    pairs = mine[0].shape[0] // frames
    block = owners * pairs
    members = block // 2
    inputs = part_ref.shape[1]
    here, section, pol = lax.axis_index("chan"), lax.axis_index("stat"), lax.axis_index("pol")
    pack(packed, 0, mine, frames)
    pack(theirs, 0, twin, frames)
    one, zero = jnp.float32(1), jnp.float32(0)

    def spread_of(slots, source, there):
        col = lax.broadcasted_iota(jnp.int32, (slots * block, 1), 0)
        slot, inner = split_low(col, block)
        k, rest = split_low(inner, pairs)
        target = (source(slot) * 2 + there(slot)) * members + (here ^ k) * (pairs // 2) + (rest >> 1)
        wide = lax.broadcasted_iota(jnp.int32, (slots * block, 2 * inputs), 1)
        return jnp.where(wide == target + (rest & 1) * inputs, one, zero).astype(jnp.bfloat16)

    near = spread_of(2, lambda slot: section, lambda slot: pol ^ slot)
    far_ref[...] = spread_of(
        2 * (sections - 1), lambda slot: section ^ ((slot >> 1) + 1), lambda slot: pol ^ (slot & 1)
    )
    height = width * block
    left = lax.broadcasted_iota(jnp.int32, (height, height), 0)
    right = lax.broadcasted_iota(jnp.int32, (1, height), 1)
    j, inner = split_low(right, block)
    k, rest = split_low(inner, pairs)
    aim = j * block + (here ^ k) * (pairs // 2) + (rest >> 1)
    part = rest & 1
    scale = jnp.float32(1)
    merge_ref[:, :height] = jnp.where(left == aim + part * members, scale, zero).astype(jnp.bfloat16)
    sign = jnp.where(part == 1, scale, -scale)
    merge_ref[:, height:] = jnp.where(left == aim + (1 - part) * members, sign, zero).astype(jnp.bfloat16)
    products = [
        jnp.concatenate([dot_tt(packed[j], packed[j]), dot_tt(packed[j], theirs[j])], 1) for j in range(width)
    ]
    part_ref[...] = settle(products, near, merge_ref[...]) * (1.0 / (frames * LANES))


def correlate_near(mine, twin, frames, sections):
    owners = len(mine)
    rows, lanes = mine[0].shape
    width, block = lanes // LANES, owners * rows // frames
    inputs = block * sections
    bf = jnp.bfloat16
    return pl.pallas_call(
        functools.partial(near_kernel, owners, sections, frames),
        out_shape=[
            jax.ShapeDtypeStruct((width * block, inputs), jnp.float32),
            jax.ShapeDtypeStruct((width, block, frames * LANES), bf),
            jax.ShapeDtypeStruct((width * block, 2 * width * block), bf),
            jax.ShapeDtypeStruct((2 * (sections - 1) * block, 2 * inputs), bf),
        ],
        in_specs=whole_vmem(2 * owners),
        out_specs=whole_vmem(4),
        scratch_shapes=[pltpu.VMEM((width, block, frames * LANES), bf)],
        compiler_params=grant(),
        name="correlate_near",
    )(*mine, *twin)


def far_products(packed, theirs, others, frames):
    for slot, blocks in enumerate(others):
        pack(theirs, slot, blocks, frames)
    return [dot_tt(packed[j], theirs[j]) for j in range(packed.shape[0])]


def gather_rows(data, blocks, owners, sections):
    rows = blocks[0].shape[0]
    here, section = lax.axis_index("chan"), lax.axis_index("stat")
    for x in range(sections):
        for k in range(owners):
            at = ((section ^ x) * owners + (here ^ k)) * rows
            data[pl.ds(pl.multiple_of(at, rows), rows), :] = blocks[x * owners + k][...]


def finish_kernel(owners, sections, frames, share, span, weight_ref, part_ref, packed, merge_ref, far_ref, *refs):
    count = owners * sections
    blocks, crossed = refs[:count], refs[count : 2 * count - owners]
    out_ref, vis_ref, data, theirs, vis, held, sems, *chunk = refs[2 * count - owners :]
    slots = held.shape[0]
    height, lanes = out_ref.shape
    steps = [(row, lane) for row in range(0, height, share) for lane in range(0, lanes, span)]
    vis_copy = pltpu.make_async_copy(vis, vis_ref, sems.at[slots])

    def copy(i):
        row, lane = steps[i]
        return pltpu.make_async_copy(
            held.at[i % slots], out_ref.at[pl.ds(row, share), pl.ds(lane, span)], sems.at[i % slots]
        )

    gather_rows(data, blocks, owners, sections)
    for i, (row, lane) in enumerate(steps):
        if i >= slots:
            copy(i - slots).wait()
        if chunk:
            load = pltpu.make_async_copy(weight_ref.at[pl.ds(row, share)], chunk[0], sems.at[slots + 1])
            load.start()
            load.wait()
            weights = chunk[0][...]
        else:
            weights = weight_ref[row : row + share, :]
        held[i % slots] = jnp.dot(weights, data[:, lane : lane + span], preferred_element_type=jnp.float32)
        copy(i).start()
        if i == min(slots, len(steps)) - 1:
            others = []
            for x in range(1, sections):
                others.append(blocks[x * owners : (x + 1) * owners])
                others.append(crossed[(x - 1) * owners : x * owners])
            products = far_products(packed, theirs, others, frames)
            vis[...] = part_ref[...] + settle(products, far_ref[...], merge_ref[...]) * (1.0 / (frames * LANES))
            vis_copy.start()
    for i in range(max(0, len(steps) - slots), len(steps)):
        copy(i).wait()
    vis_copy.wait()


def finish(weights, near, mine, others, crossed, frames, sections):
    owners = len(mine)
    height, depth = weights.shape
    _, lanes = mine[0].shape
    part, packed, merge, far = near
    width, block, length = packed.shape
    resident = height * depth * 2 <= RESIDENT
    span = min(lanes, 512)
    share = 8 * pieces(height // 8, 100 if resident else 25)
    slots = 4
    weight_spec = pl.BlockSpec(memory_space=pltpu.VMEM if resident else pltpu.HBM)
    chunk = [] if resident else [pltpu.VMEM((share, depth), jnp.bfloat16)]
    return pl.pallas_call(
        functools.partial(finish_kernel, owners, sections, frames, share, span),
        out_shape=[jax.ShapeDtypeStruct((height, lanes), jnp.float32), jax.ShapeDtypeStruct(part.shape, jnp.float32)],
        in_specs=[weight_spec] + whole_vmem(4 + 2 * len(others) + owners),
        out_specs=[pl.BlockSpec(memory_space=pl.ANY)] * 2,
        scratch_shapes=[
            pltpu.VMEM((depth, lanes), jnp.bfloat16),
            pltpu.VMEM((width, 2 * (sections - 1) * block, length), jnp.bfloat16),
            pltpu.VMEM(part.shape, jnp.float32),
            pltpu.VMEM((slots, share, span), jnp.float32),
            pltpu.SemaphoreType.DMA((slots + 2,)),
        ]
        + chunk,
        compiler_params=grant() if resident else None,
        name="finish",
    )(weights, part, packed, merge, far, *mine, *others, *crossed)


def partner(x, axis, distance):
    return lax.ppermute(x, axis, [(i, i ^ distance) for i in range(lax.axis_size(axis))])


def moved(parts, axis, distance):
    if len(parts) == 1:
        return [partner(parts[0], axis, distance)]
    return jnp.split(partner(jnp.concatenate(parts, 0), axis, distance), len(parts), 0)


def on_device(voltages, filter_taps, beam_table, beam_index, block_owner):
    owners, sections = lax.axis_size("chan"), lax.axis_size("stat")
    stations = voltages.shape[1]
    frames = voltages.shape[3] - filter_taps.shape[0] + 1
    pairs = 2 * stations
    groups = block_owner.shape[0]
    owned = beam_index.shape[0] // sections
    tables = weight_inputs(beam_table, beam_index, frames, pairs)
    lead = max(1, owners // 4)
    paired = int(lead == 1)
    own = channelise(voltages, filter_taps, block_owner, owners, paired, tables)
    pair, tables = own[owners], own[owners + paired :]
    weights = framed_weights(tables, frames, pairs, owned)
    mine = [own[0]] + [partner(own[k], "chan", k) for k in range(1, owners)]
    twin, others, crossed = [], [[] for _ in range(1, sections)], [[] for _ in range(1, sections)]
    for g in range(owners // lead):
        part = mine[g * lead : (g + 1) * lead]
        twin += moved(part, "pol", 1)
        for x in range(1, sections):
            if paired and g == 0:
                both = partner(pair, "stat", x)
                rows = both.shape[0] // 2
                far, later = [both[:rows]], partner(both[rows:], "chan", 1)
            elif paired and g == 1:
                far = [later]
            else:
                far = moved(part, "stat", x)
            others[x - 1] += far
            crossed[x - 1] += moved(far, "pol", 1)
    near = correlate_near(mine, twin, frames, sections)
    beams, vis = finish(weights, near, mine, sum(others, []), sum(crossed, []), frames, sections)
    vis = vis.reshape(groups // owners, 2, -1, vis.shape[1])
    return vis, beams.reshape(owned, 1, 2, frames, -1)


def solution(mesh):
    return jax.shard_map(
        on_device,
        mesh=mesh,
        in_specs=(P(("group", "stat"), "chan", "pol", None, None, None), P(), P(), P(), P()),
        out_specs=(
            P(("group", "chan"), None, ("stat", "pol"), None),
            P(("group", "stat"), "pol", None, None, "chan"),
        ),
        check_vma=False,
    )
```

```python
import functools, math
import jax, jax.numpy as jnp, numpy as np
from jax import lax
from jax.experimental import pallas as pl
from jax.experimental.pallas import tpu as pltpu
from jax.sharding import PartitionSpec as P


LANES = 128
HALF = 4


def dft_parts(rows, cols, length):
    phase = np.outer(np.arange(rows), np.arange(cols)) % length * (2.0 * np.pi / length)
    return np.cos(phase), np.sin(phase)


def channel_tables(nfft, groups):
    depth = nfft // LANES
    per_group = LANES // depth
    cosine, sine = dft_parts(depth, depth, depth)
    pair = np.stack([np.stack([cosine, sine], -1), np.stack([-sine, cosine], -1)])
    first = np.einsum("akrc,fg->afkgrc", pair, np.eye(HALF))
    first = first.reshape(2 * HALF * depth, HALF * depth * 2)
    turn_cos, turn_sin = dft_parts(depth, LANES, nfft)
    cosine, sine = dft_parts(LANES, LANES, LANES)
    order = (np.arange(groups)[None, :] * per_group + np.arange(per_group)[:, None]).reshape(-1)
    cosine, sine = cosine[order] / math.sqrt(nfft), sine[order] / math.sqrt(nfft)
    second = np.concatenate([np.concatenate([cosine, sine], 1), np.concatenate([-sine, cosine], 1)], 0)
    spread = np.einsum("qr,fg,kl->qfkgrl", np.eye(per_group), np.eye(HALF), np.eye(depth))
    spread = spread.reshape(per_group * HALF * depth, HALF * per_group * depth)
    bf = lambda x: jnp.asarray(x, jnp.bfloat16)
    return bf(first), jnp.asarray(np.stack([turn_cos, turn_sin]), jnp.float32), bf(second), bf(spread)


def channel_kernel(owners, paired, owner_hbm, volt_ref, taps_hbm, first_ref, turn_ref, second_ref, spread_ref, *rest):
    passed, outs, handed = rest[:3], rest[3 : 3 + owners + paired], rest[3 + owners + paired : 6 + owners + paired]
    owner_ref, volts, taps_ref, tap_rows, first, turn, second, spread, filt, wide, pick, sems = rest[6 + owners + paired :]
    stations, blocks, rows, _ = volt_ref.shape
    taps = taps_ref.shape[0]
    frames = blocks - taps + 1
    halves = frames // HALF
    depth = rows // 2
    groups = owner_hbm.shape[0]
    width = groups // owners
    quads = LANES // depth
    span = HALF * depth
    here = lax.axis_index("chan")
    tap_copy = pltpu.make_async_copy(taps_hbm, taps_ref, sems.at[stations + 4])
    tap_copy.start()
    owner_copy = pltpu.make_async_copy(owner_hbm, owner_ref, sems.at[stations + 5])
    owner_copy.start()
    copies = []
    for s in range(stations):
        copies.append(pltpu.make_async_copy(volt_ref.at[s], volts.at[s], sems.at[s]))
    consts = []
    for i, (src, dst) in enumerate([(first_ref, first), (turn_ref, turn), (second_ref, second), (spread_ref, spread)]):
        consts.append(pltpu.make_async_copy(src, dst, sems.at[stations + i]))
    for i, (src, dst) in enumerate(zip(passed, handed)):
        consts.append(pltpu.make_async_copy(src, dst, sems.at[stations + 6 + i]))
    for c in copies + consts:
        c.start()
    tap_copy.wait()

    sub = lax.broadcasted_iota(jnp.int32, (8, LANES), 0)
    for t in range(taps):
        for m in range(rows // 8):
            parts = [jnp.broadcast_to(taps_ref[t : t + 1, pl.ds((4 * m + i) * LANES, LANES)], (8, LANES)) for i in range(4)]
            low = jnp.where(sub < 2, parts[0], parts[1])
            high = jnp.where(sub < 6, parts[2], parts[3])
            tap_rows[t, pl.ds(8 * m, 8), :] = jnp.where(sub < 4, low, high)

    owner_copy.wait()
    sc = 2 * stations
    lane = lax.broadcasted_iota(jnp.int32, (sc, sc * groups), 1)
    base = lax.broadcasted_iota(jnp.int32, (sc, sc * groups), 0) * groups
    for k in range(owners):
        for j in range(width):
            g = owner_ref[(here ^ k) * width + j]
            p = (k * width + j) * sc
            pick[pl.ds(p, sc), :] = jnp.where(lane == base + g, 1.0, 0.0).astype(jnp.bfloat16)

    step = 16
    for s in range(stations):
        copies[s].wait()

        def fir(m, carry, s=s):
            at = pl.multiple_of(m * step, step)
            x = [volts[s, b, pl.ds(at, step), :].astype(jnp.float32) for b in range(blocks)]
            w = [tap_rows[t, pl.ds(at, step), :] for t in range(taps)]
            for f in range(frames):
                total = w[0] * x[f]
                for t in range(1, taps):
                    total = total + w[t] * x[f + t]
                row = pl.multiple_of((f % HALF) * rows + at, step)
                filt[s, pl.ds(row, step), pl.ds((f // HALF) * LANES, LANES)] = total.astype(jnp.bfloat16)
            return carry

        lax.fori_loop(0, rows // step, fir, 0)

    for c in consts:
        c.wait()
    f32 = jnp.float32
    cosine = jnp.concatenate([turn[0]] * HALF, 0)
    sine = jnp.concatenate([turn[1]] * HALF, 0)
    for s in range(stations):
        y = jnp.dot(first[...], filt[s], preferred_element_type=f32)
        re, im = y[:span], y[span:]
        turned = []
        for h in range(halves):
            a, b = re[:, h * LANES : (h + 1) * LANES], im[:, h * LANES : (h + 1) * LANES]
            turned.append(jnp.concatenate([a * cosine + b * sine, b * cosine - a * sine], 1))
        turned = jnp.concatenate(turned, 0).astype(jnp.bfloat16)
        z = lax.dot_general(second[...], turned, (((1,), (1,)), ((), ())), preferred_element_type=f32).astype(jnp.bfloat16)
        for c in range(2):
            for q in range(quads):
                for h in range(halves):
                    wide[h, pl.ds((s * 2 + c) * groups, groups), pl.ds(q * LANES, LANES)] = z[
                        c * quads * groups + q * groups : c * quads * groups + (q + 1) * groups, h * LANES : (h + 1) * LANES
                    ]
    for h in range(halves):
        y = jnp.dot(wide[h], spread[...], preferred_element_type=f32).astype(jnp.bfloat16)
        z = jnp.dot(pick[...], y, preferred_element_type=f32)
        for k in range(owners):
            for j in range(width):
                for f in range(HALF):
                    p = (k * width + j) * sc
                    block = z[p : p + sc, f * LANES : (f + 1) * LANES].astype(jnp.bfloat16)
                    row = (h * HALF + f) * sc
                    outs[k][pl.ds(row, sc), pl.ds(j * LANES, LANES)] = block
                    if paired and k < 2:
                        outs[owners][pl.ds(k * frames * sc + row, sc), pl.ds(j * LANES, LANES)] = block


def channelise(voltages, filter_taps, block_owner, owners, paired, passed):
    _, stations, _, blocks, _, nfft = voltages.shape
    taps = filter_taps.shape[0]
    frames = blocks - taps + 1
    groups = block_owner.shape[0]
    depth = nfft // LANES
    volts = voltages.reshape(stations, blocks, 2, depth, LANES).transpose(0, 1, 3, 2, 4).reshape(stations, blocks, 2 * depth, LANES)
    first, turn, second, spread = channel_tables(nfft, groups)
    sc = 2 * stations
    width = groups // owners
    inputs = (block_owner, volts, filter_taps, first, turn, second, spread, *passed)
    block = jax.ShapeDtypeStruct((frames * sc, width * LANES), jnp.bfloat16)
    pair = jax.ShapeDtypeStruct((2 * frames * sc, width * LANES), jnp.bfloat16)
    anyspec = pl.BlockSpec(memory_space=pltpu.HBM)
    bf = jnp.bfloat16
    return pl.pallas_call(
        functools.partial(channel_kernel, owners, paired),
        out_shape=[block] * owners + [pair] * paired + [jax.ShapeDtypeStruct(x.shape, x.dtype) for x in passed],
        in_specs=[anyspec] * len(inputs),
        out_specs=[pl.BlockSpec(memory_space=pltpu.VMEM)] * (owners + paired + len(passed)),
        scratch_shapes=[
            pltpu.SMEM(block_owner.shape, jnp.int32),
            pltpu.VMEM(volts.shape, bf),
            pltpu.VMEM(filter_taps.shape, jnp.float32),
            pltpu.VMEM((taps, 2 * depth, LANES), jnp.float32),
            pltpu.VMEM(first.shape, bf),
            pltpu.VMEM(turn.shape, jnp.float32),
            pltpu.VMEM(second.shape, bf),
            pltpu.VMEM(spread.shape, bf),
            pltpu.VMEM((stations, HALF * 2 * depth, frames // HALF * LANES), bf),
            pltpu.VMEM((frames // HALF, sc * groups, spread.shape[0]), bf),
            pltpu.VMEM((groups * sc, sc * groups), bf),
            pltpu.SemaphoreType.DMA((stations + 9,)),
        ],
        compiler_params=grant(),
        name="channelise",
    )(*[pltpu.with_memory_space_constraint(x, pltpu.HBM) for x in inputs])


VMEM_BYTES = 24 * 2**20
RESIDENT = 8 * 2**20
SLICE = 32


def whole_vmem(count):
    return [pl.BlockSpec(memory_space=pltpu.VMEM)] * count


def grant(size=VMEM_BYTES):
    return pltpu.CompilerParams(vmem_limit_bytes=size)


def pieces(total, most):
    return max(d for d in range(1, most + 1) if total % d == 0)


def split_low(x, size):
    shift = size.bit_length() - 1
    assert size == 1 << shift
    return x >> shift, x & (size - 1)


def bf_pair(x):
    high = x.astype(jnp.bfloat16)
    return high, (x - high.astype(jnp.float32)).astype(jnp.bfloat16)


def dot_tt(a, b):
    return lax.dot_general(a, b, (((1,), (1,)), ((), ())), preferred_element_type=jnp.float32)


def weights_kernel(pairs, owned, share, table_ref, index_ref, copy_ref, out_ref, rows_ref):
    stations, beams = index_ref.shape
    tile, spread = copy_ref.shape
    frames = spread // tile
    count = 2 * owned
    start = lax.axis_index("stat") * owned
    factor = 1.0 / math.sqrt(stations)

    def prepare():
        row = lax.broadcasted_iota(jnp.int32, (count, beams), 0)
        lane = lax.broadcasted_iota(jnp.int32, (count, beams), 1)
        hit = lane == start + (row >> 1)
        one, zero = jnp.float32(1), jnp.float32(0)
        choose = [jnp.where(hit & ((row & 1) == c), one, zero).astype(jnp.bfloat16) for c in range(2)]
        for i in range(stations // SLICE):
            index = index_ref[i * SLICE : (i + 1) * SLICE, :]
            real = jnp.zeros(index.shape, jnp.float32)
            imag = jnp.zeros(index.shape, jnp.float32)
            for e in range(table_ref.shape[1]):
                here = index == e
                real = jnp.where(here, jnp.broadcast_to(table_ref[0:1, e : e + 1], index.shape), real)
                imag = jnp.where(here, jnp.broadcast_to(table_ref[1:2, e : e + 1], index.shape), imag)
            real, imag = real * factor, imag * factor
            upper = jnp.concatenate([real, -imag], 0).astype(jnp.bfloat16)
            lower = jnp.concatenate([imag, real], 0).astype(jnp.bfloat16)
            w = dot_tt(choose[0], upper) + dot_tt(choose[1], lower)
            rows_ref[:, i * spread : (i + 1) * spread] = jnp.dot(
                w.astype(jnp.bfloat16), copy_ref[...], preferred_element_type=jnp.float32
            )

    first = 0
    if share == count:
        prepare()
    else:
        pl.when(pl.program_id(0) == 0)(prepare)
        first = pl.program_id(0) * share
    width = out_ref.shape[1]
    lane = lax.broadcasted_iota(jnp.int32, (frames, width), 1)
    mine = split_low(split_low(lane, pairs)[0], frames)[1] == lax.broadcasted_iota(jnp.int32, (frames, width), 0)

    def fill(i, carry):
        row = rows_ref[pl.ds(first + i, 1), :]
        out_ref[pl.ds(pl.multiple_of(i * frames, frames), frames), :] = jnp.where(
            mine, jnp.broadcast_to(row, (frames, width)), 0.0
        ).astype(jnp.bfloat16)
        return carry

    lax.fori_loop(0, share, fill, 0, unroll=pieces(share, 10))


def weight_inputs(beam_table, beam_index, frames, pairs):
    eye = np.eye
    copies = np.einsum("bp,sq,ct,f->cbspqft", eye(2 * SLICE // pairs), eye(pairs // 2), eye(2), np.ones(frames))
    copies = np.moveaxis(copies, (3, 5, 4, 6), (3, 4, 5, 6)).reshape(2 * SLICE, 2 * SLICE * frames)
    return beam_table, beam_index.T, jnp.asarray(copies, jnp.bfloat16)


def framed_weights(inputs, frames, pairs, owned):
    stations = inputs[1].shape[0]
    depth = 2 * stations * frames
    count = 2 * owned
    resident = count * frames * depth * 2 <= RESIDENT
    share = count if resident else pieces(count, 10)
    extra = {}
    if not resident:
        extra = dict(grid=(count // share,), out_specs=pl.BlockSpec((share * frames, depth), lambda i: (i, 0)))
    return pl.pallas_call(
        functools.partial(weights_kernel, pairs, owned, share),
        out_shape=jax.ShapeDtypeStruct((count * frames, depth), jnp.bfloat16),
        in_specs=whole_vmem(3),
        scratch_shapes=[pltpu.VMEM((count, depth), jnp.float32)],
        compiler_params=grant() if resident else None,
        name="framed_weights",
        **extra,
    )(*inputs)


def pack(packed, slot, blocks, frames):
    rows, lanes = blocks[0].shape
    pairs = rows // frames
    for k, ref in enumerate(blocks):
        at = (slot * len(blocks) + k) * pairs
        for j in range(lanes // LANES):
            for f in range(frames):
                packed[j, pl.ds(at, pairs), pl.ds(f * LANES, LANES)] = ref[
                    pl.ds(f * pairs, pairs), pl.ds(j * LANES, LANES)
                ]


def settle(products, spread, merge):
    inputs = spread.shape[1] // 2
    v = bf_pair(jnp.concatenate(products, 0))
    u = sum(jnp.dot(x, spread, preferred_element_type=jnp.float32) for x in v)
    u = bf_pair(jnp.concatenate([u[:, :inputs], u[:, inputs:]], 0))
    return sum(jnp.dot(merge, x, preferred_element_type=jnp.float32) for x in u)


def near_kernel(owners, sections, frames, *refs):
    mine, twin = refs[:owners], refs[owners : 2 * owners]
    part_ref, packed, merge_ref, far_ref, theirs = refs[2 * owners :]
    width = packed.shape[0]
    pairs = mine[0].shape[0] // frames
    block = owners * pairs
    members = block // 2
    inputs = part_ref.shape[1]
    here, section, pol = lax.axis_index("chan"), lax.axis_index("stat"), lax.axis_index("pol")
    pack(packed, 0, mine, frames)
    pack(theirs, 0, twin, frames)
    one, zero = jnp.float32(1), jnp.float32(0)

    def spread_of(slots, source, there):
        col = lax.broadcasted_iota(jnp.int32, (slots * block, 1), 0)
        slot, inner = split_low(col, block)
        k, rest = split_low(inner, pairs)
        target = (source(slot) * 2 + there(slot)) * members + (here ^ k) * (pairs // 2) + (rest >> 1)
        wide = lax.broadcasted_iota(jnp.int32, (slots * block, 2 * inputs), 1)
        return jnp.where(wide == target + (rest & 1) * inputs, one, zero).astype(jnp.bfloat16)

    near = spread_of(2, lambda slot: section, lambda slot: pol ^ slot)
    far_ref[...] = spread_of(
        2 * (sections - 1), lambda slot: section ^ ((slot >> 1) + 1), lambda slot: pol ^ (slot & 1)
    )
    height = width * block
    left = lax.broadcasted_iota(jnp.int32, (height, height), 0)
    right = lax.broadcasted_iota(jnp.int32, (1, height), 1)
    j, inner = split_low(right, block)
    k, rest = split_low(inner, pairs)
    aim = j * block + (here ^ k) * (pairs // 2) + (rest >> 1)
    part = rest & 1
    scale = jnp.float32(1)
    merge_ref[:, :height] = jnp.where(left == aim + part * members, scale, zero).astype(jnp.bfloat16)
    sign = jnp.where(part == 1, scale, -scale)
    merge_ref[:, height:] = jnp.where(left == aim + (1 - part) * members, sign, zero).astype(jnp.bfloat16)
    products = [
        jnp.concatenate([dot_tt(packed[j], packed[j]), dot_tt(packed[j], theirs[j])], 1) for j in range(width)
    ]
    part_ref[...] = settle(products, near, merge_ref[...]) * (1.0 / (frames * LANES))


def correlate_near(mine, twin, frames, sections):
    owners = len(mine)
    rows, lanes = mine[0].shape
    width, block = lanes // LANES, owners * rows // frames
    inputs = block * sections
    bf = jnp.bfloat16
    return pl.pallas_call(
        functools.partial(near_kernel, owners, sections, frames),
        out_shape=[
            jax.ShapeDtypeStruct((width * block, inputs), jnp.float32),
            jax.ShapeDtypeStruct((width, block, frames * LANES), bf),
            jax.ShapeDtypeStruct((width * block, 2 * width * block), bf),
            jax.ShapeDtypeStruct((2 * (sections - 1) * block, 2 * inputs), bf),
        ],
        in_specs=whole_vmem(2 * owners),
        out_specs=whole_vmem(4),
        scratch_shapes=[pltpu.VMEM((width, block, frames * LANES), bf)],
        compiler_params=grant(),
        name="correlate_near",
    )(*mine, *twin)


def far_products(packed, theirs, others, frames):
    for slot, blocks in enumerate(others):
        pack(theirs, slot, blocks, frames)
    return [dot_tt(packed[j], theirs[j]) for j in range(packed.shape[0])]


def gather_rows(data, blocks, owners, sections):
    rows = blocks[0].shape[0]
    here, section = lax.axis_index("chan"), lax.axis_index("stat")
    for x in range(sections):
        for k in range(owners):
            at = ((section ^ x) * owners + (here ^ k)) * rows
            data[pl.ds(pl.multiple_of(at, rows), rows), :] = blocks[x * owners + k][...]


def finish_kernel(owners, sections, frames, strips, span, weight_ref, part_ref, packed, merge_ref, far_ref, *refs):
    count = owners * sections
    blocks, crossed = refs[:count], refs[count : 2 * count - owners]
    out_ref, vis_ref, data, theirs, vis, held, sems, *chunk = refs[2 * count - owners :]
    slots = held.shape[0]
    _, lanes = out_ref.shape
    steps = []
    for lane in range(0, lanes, span):
        row = 0
        for size in strips if lane == 0 else strips[::-1]:
            steps.append((row, size, lane))
            row += size
    vis_copy = pltpu.make_async_copy(vis, vis_ref, sems.at[slots])

    def copy(i):
        row, size, lane = steps[i]
        return pltpu.make_async_copy(
            held.at[i % slots, pl.ds(0, size)], out_ref.at[pl.ds(row, size), pl.ds(lane, span)], sems.at[i % slots]
        )

    gather_rows(data, blocks, owners, sections)
    for i, (row, size, lane) in enumerate(steps):
        if i >= slots:
            copy(i - slots).wait()
        if chunk:
            load = pltpu.make_async_copy(weight_ref.at[pl.ds(row, size)], chunk[0].at[pl.ds(0, size)], sems.at[slots + 1])
            load.start()
            load.wait()
            weights = chunk[0][:size]
        else:
            weights = weight_ref[row : row + size, :]
        held[i % slots, :size] = jnp.dot(weights, data[:, lane : lane + span], preferred_element_type=jnp.float32)
        copy(i).start()
        if i == min(slots + 1, len(steps) - 1):
            others = []
            for x in range(1, sections):
                others.append(blocks[x * owners : (x + 1) * owners])
                others.append(crossed[(x - 1) * owners : x * owners])
            products = far_products(packed, theirs, others, frames)
            vis[...] = part_ref[...] + settle(products, far_ref[...], merge_ref[...]) * (1.0 / (frames * LANES))
            vis_copy.start()
    for i in range(max(0, len(steps) - slots), len(steps)):
        copy(i).wait()
    vis_copy.wait()


def finish(weights, near, mine, others, crossed, frames, sections):
    owners = len(mine)
    height, depth = weights.shape
    _, lanes = mine[0].shape
    part, packed, merge, far = near
    width, block, length = packed.shape
    resident = height * depth * 2 <= RESIDENT
    span = min(lanes, 512)
    lead = height // 80 * 8
    third = (height - lead) // 24 * 8
    strips = [lead, third, third, height - lead - 2 * third]
    if not resident:
        strips = [8 * pieces(height // 8, 25)] * (height // 8 // pieces(height // 8, 25))
    share = max(strips)
    slots = 4
    weight_spec = pl.BlockSpec(memory_space=pltpu.VMEM if resident else pltpu.HBM)
    chunk = [] if resident else [pltpu.VMEM((share, depth), jnp.bfloat16)]
    return pl.pallas_call(
        functools.partial(finish_kernel, owners, sections, frames, strips, span),
        out_shape=[jax.ShapeDtypeStruct((height, lanes), jnp.float32), jax.ShapeDtypeStruct(part.shape, jnp.float32)],
        in_specs=[weight_spec] + whole_vmem(4 + 2 * len(others) + owners),
        out_specs=[pl.BlockSpec(memory_space=pl.ANY)] * 2,
        scratch_shapes=[
            pltpu.VMEM((depth, lanes), jnp.bfloat16),
            pltpu.VMEM((width, 2 * (sections - 1) * block, length), jnp.bfloat16),
            pltpu.VMEM(part.shape, jnp.float32),
            pltpu.VMEM((slots, share, span), jnp.float32),
            pltpu.SemaphoreType.DMA((slots + 2,)),
        ]
        + chunk,
        compiler_params=grant() if resident else None,
        name="finish",
    )(weights, part, packed, merge, far, *mine, *others, *crossed)


def partner(x, axis, distance):
    return lax.ppermute(x, axis, [(i, i ^ distance) for i in range(lax.axis_size(axis))])


def moved(parts, axis, distance):
    if len(parts) == 1:
        return [partner(parts[0], axis, distance)]
    return jnp.split(partner(jnp.concatenate(parts, 0), axis, distance), len(parts), 0)


def on_device(voltages, filter_taps, beam_table, beam_index, block_owner):
    owners, sections = lax.axis_size("chan"), lax.axis_size("stat")
    stations = voltages.shape[1]
    frames = voltages.shape[3] - filter_taps.shape[0] + 1
    pairs = 2 * stations
    groups = block_owner.shape[0]
    owned = beam_index.shape[0] // sections
    tables = weight_inputs(beam_table, beam_index, frames, pairs)
    lead = max(1, owners // 4)
    paired = int(lead == 1)
    own = channelise(voltages, filter_taps, block_owner, owners, paired, tables)
    pair, tables = own[owners], own[owners + paired :]
    weights = framed_weights(tables, frames, pairs, owned)
    mine = [own[0]] + [partner(own[k], "chan", k) for k in range(1, owners)]
    twin, others, crossed = [], [[] for _ in range(1, sections)], [[] for _ in range(1, sections)]
    for g in range(owners // lead):
        part = mine[g * lead : (g + 1) * lead]
        twin += moved(part, "pol", 1)
        for x in range(1, sections):
            if paired and g == 0:
                both = partner(pair, "stat", x)
                rows = both.shape[0] // 2
                far, later = [both[:rows]], partner(both[rows:], "chan", 1)
            elif paired and g == 1:
                far = [later]
            else:
                far = moved(part, "stat", x)
            others[x - 1] += far
            crossed[x - 1] += moved(far, "pol", 1)
    near = correlate_near(mine, twin, frames, sections)
    beams, vis = finish(weights, near, mine, sum(others, []), sum(crossed, []), frames, sections)
    vis = vis.reshape(groups // owners, 2, -1, vis.shape[1])
    return vis, beams.reshape(owned, 1, 2, frames, -1)


def solution(mesh):
    return jax.shard_map(
        on_device,
        mesh=mesh,
        in_specs=(P(("group", "stat"), "chan", "pol", None, None, None), P(), P(), P(), P()),
        out_specs=(
            P(("group", "chan"), None, ("stat", "pol"), None),
            P(("group", "stat"), "pol", None, None, "chan"),
        ),
        check_vma=False,
    )
```
